32 devices in a mesh: field: 2 (over core), group: 2 (over y), row: 8 (over z, x).
Axes of the slice: x: 2, y: 2, z: 4, core: 2. Of those that a mesh axis runs over, the one named last changes fastest.
Arguments:
- anomalies: bfloat16 [2, 16384, 512], P('field', ('group', 'row')), may hold values from -6 to 6
- valid_rows: int32 [2, 16], P('field', ('group', 'row')), may hold values from 512 to 1024
- start_basis: float32 [512, 64], replicated, may hold values from -6 to 6
Outputs:
- patterns: float32 [2, 16384, 64], P('field', ('group', 'row'))
- strengths: float32 [64], replicated
The draws below stay inside these ranges and needn't reach their ends.
Inputs may be any that keep to these rules, and one draw needn't show every extreme that they name: `valid_rows`: the number of ocean points at the head of each shard; the rest of the shard is land and holds values that must be ignored.
All inputs are finite; a program needn't handle non-finite values.
Results may differ from the reference program's by a relative error of at most 0.0003.
Values sent between devices are 32-bit elements; how exact they have to be, the bound alone decides.
No kernel may reach another device: no remote copies, remote signals or barrier semaphores. Data moves between devices by JAX's collectives and lax.ppermute only.
A program may use at most 64 MiB of HBM per device.

```python
import math
import jax
import jax.numpy as jnp
from jax import lax

MONTHS = 512
MODES = 64
ROWS_DEV = 1024
ITERS = 1
SHARDS = 16
ROWS = 16384


def one_field(field_key):
    pieces = jax.random.split(field_key, 2)
    white_noise = jax.random.normal(pieces[0], (ROWS, MONTHS + 2), jnp.float32)
    smoothed = (white_noise[:, 2:] + 0.6 * white_noise[:, 1:-1] + 0.4 * white_noise[:, :-2]) / math.sqrt(1.52)
    month_scale = jnp.exp(jax.random.uniform(pieces[1], (1, MONTHS), jnp.float32, math.log(0.5), math.log(2.0)))
    values = smoothed * month_scale
    return jnp.clip(values, -6.0, 6.0)


def draw_anomalies(key, part):
    field_keys = jax.random.split(jax.random.fold_in(key, 17), 2)
    return lax.map(one_field, field_keys).astype(jnp.bfloat16)


def set_ends(result, key, low, largest):
    longest = result.shape.index(max(result.shape))
    spots = []
    for shift in (0, 1):
        where = [jax.random.randint(jax.random.fold_in(key, axis), (), 0, length) for axis, length in enumerate(result.shape)]
        where[longest] = (where[longest] + shift) % result.shape[longest]
        spots.append(tuple(where))
    return result.at[spots[0]].set(low).at[spots[1]].set(largest)


def bell_draw(stream_key, shape, width, reach, kind=jnp.bfloat16):
    array = width * jax.random.normal(stream_key, shape, jnp.float32)
    return jnp.clip(array, min=-reach, max=reach).astype(kind)


def setup_inputs(seed: int = 0) -> dict:
    seeds = jax.random.split(jax.random.key(seed), 4)
    anomalies = draw_anomalies(jax.random.fold_in(seeds[3], 71), 0)
    valid_rows = set_ends(jax.random.randint(seeds[1], (2, SHARDS), ROWS_DEV // 2, ROWS_DEV + 1), jax.random.fold_in(seeds[1], 1), ROWS_DEV // 2, ROWS_DEV).astype(jnp.int32)
    start_basis = bell_draw(seeds[2], (MONTHS, MODES), 1.0, 6.0, jnp.float32)
    return {"anomalies": anomalies, "valid_rows": valid_rows, "start_basis": start_basis}


HIGH = lax.Precision.HIGHEST

def orthonormal(block):
    product = jnp.dot(block.T.astype(jnp.float32), block.astype(jnp.float32), precision=HIGH, preferred_element_type=jnp.float32)
    lower = jnp.linalg.cholesky(product)
    return lax.linalg.triangular_solve(lower, block, left_side=False, lower=True, transpose_a=True)

def masked_field(values, counts):
    index = jnp.arange(ROWS, dtype=jnp.int32)
    shard = index // ROWS_DEV
    place = index - shard * ROWS_DEV
    keep = place < counts[shard]
    return jnp.where(keep[:, None], values, jnp.zeros_like(values))

def upper_factor(masked, counts):
    gram = lax.dot_general(masked.astype(jnp.float32), masked.astype(jnp.float32), (((0,), (0,)), ((), ())), preferred_element_type=jnp.float32)
    total = jnp.sum(counts.astype(jnp.float32))
    return jnp.linalg.cholesky(gram / total).T

def project(masked, factor, basis):
    solved = lax.linalg.triangular_solve(factor, basis, left_side=True, lower=False)
    blocks = masked.reshape(SHARDS, ROWS_DEV, MONTHS)
    out = lax.map(lambda piece: jnp.dot(piece.astype(jnp.float32), solved.astype(jnp.float32), precision=HIGH, preferred_element_type=jnp.float32), blocks)
    return out.reshape(ROWS, MODES)

def reference(anomalies, valid_rows, start_basis):
    first = masked_field(anomalies[0], valid_rows[0])
    second = masked_field(anomalies[1], valid_rows[1])
    factor_one = upper_factor(first, valid_rows[0])
    factor_two = upper_factor(second, valid_rows[1])
    coupling = jnp.dot(factor_one.astype(jnp.float32), factor_two.T.astype(jnp.float32), precision=HIGH, preferred_element_type=jnp.float32)
    right = start_basis
    left = start_basis
    for step in range(ITERS):
        left = orthonormal(jnp.dot(coupling.astype(jnp.float32), right.astype(jnp.float32), precision=HIGH, preferred_element_type=jnp.float32))
        right = orthonormal(jnp.dot(coupling.T.astype(jnp.float32), left.astype(jnp.float32), precision=HIGH, preferred_element_type=jnp.float32))
    image = jnp.dot(coupling.astype(jnp.float32), right.astype(jnp.float32), precision=HIGH, preferred_element_type=jnp.float32)
    strengths = jnp.sum(left * image, axis=0)
    patterns = jnp.stack([project(first, factor_one, left), project(second, factor_two, right)])
    return (patterns, strengths)
```

```python
import functools
import math

import jax
import jax.numpy as jnp
from jax import lax
from jax.experimental import pallas as pl
from jax.experimental.pallas import tpu as pltpu
from jax.sharding import PartitionSpec as P

HIGH = lax.Precision.HIGHEST
F32 = jnp.float32
BLOCK = 128
TILE = 8
VMEM = pl.BlockSpec(memory_space=pltpu.VMEM)
SMEM = pl.BlockSpec(memory_space=pltpu.SMEM)


def dot(a, b, ca=1, cb=0):
    return lax.dot_general(
        a, b, (((ca,), (cb,)), ((), ())), precision=HIGH, preferred_element_type=F32
    )


def lane_copy(tile, lane):
    return jnp.broadcast_to(tile[:, lane : lane + 1], tile.shape)


def row_copy(tile, row):
    return jnp.broadcast_to(tile[row : row + 1, :], tile.shape)


def factor_block(a_ref, u_ref, steps):
    lane = lax.broadcasted_iota(jnp.int32, (TILE, BLOCK), 1)
    sub = lax.broadcasted_iota(jnp.int32, (TILE, BLOCK), 0)
    for s in range(steps):
        k = TILE * s
        tile = a_ref[k : k + TILE, :]
        cols = [lane_copy(tile, k + j) for j in range(TILE)]
        e = {(i, j): row_copy(cols[j], i) for j in range(TILE) for i in range(j, TILE)}
        inside = (lane >= k) & (lane < k + TILE)
        scale, low = [], {}
        for j in range(TILE):
            scale.append(lax.rsqrt(e[j, j]))
            for i in range(j + 1, TILE):
                low[i, j] = e[i, j] * scale[j]
            for i in range(j + 1, TILE):
                for m in range(j + 1, i + 1):
                    e[i, m] = e[i, m] - low[i, j] * low[m, j]
        rows, uppers = [], []
        for i in range(TILE):
            upper = row_copy(tile, i)
            row = jnp.where(inside, jnp.where(lane == k + i, 1.0, 0.0), upper)
            for m in range(i):
                row = row - low[i, m] * rows[m]
                upper = upper - low[i, m] * uppers[m]
            rows.append(row * scale[i])
            uppers.append(upper * scale[i])
        new, up = rows[0], uppers[0]
        for i in range(1, TILE):
            new = jnp.where(sub == i, rows[i], new)
            up = jnp.where(sub == i, uppers[i], up)
        a_ref[k : k + TILE, :] = new
        u_ref[k : k + TILE, :] = jnp.where(lane >= k + sub, up, 0.0)
        for g in range(s + 1, steps):
            q = TILE * g
            t = a_ref[q : q + TILE, :]
            w = []
            for j in range(TILE):
                acc = lane_copy(t, k + j)
                for m in range(j):
                    acc = acc - low[j, m] * w[m]
                w.append(acc * scale[j])
            t = jnp.where(inside, 0.0, t)
            for i in range(TILE):
                t = t - w[i] * rows[i]
            a_ref[q : q + TILE, :] = t


def lower_part(x):
    row = lax.broadcasted_iota(jnp.int32, x.shape, 0)
    lane = lax.broadcasted_iota(jnp.int32, x.shape, 1)
    return jnp.where(lane <= row, x, 0.0)


def pairs(nb):
    return [(i, j) for i in range(nb) for j in range(i, nb)]


def read_half(packed_ref, quarter, start):
    p, o = divmod(start, quarter)
    return packed_ref[p, o : o + 64, :]


def unpack(packed_ref, nb, put):
    quarter = packed_ref.shape[1] - TILE
    inverse = 1.0 / packed_ref[0, quarter : quarter + 1, :]
    for t, (i, j) in enumerate(pairs(nb)):
        for h in range(2):
            put(i, j, h, read_half(packed_ref, quarter, t * BLOCK + 64 * h) * inverse)


def factor_kernel(packed_ref, x_ref, y_ref, s_ref, u_ref, d_ref, ud_ref):
    n = x_ref.shape[0]
    nb = n // BLOCK
    u_ref[...] = jnp.zeros_like(u_ref)

    def put(i, j, h, v):
        r = i * BLOCK + h * 64
        s_ref[r : r + 64, j * BLOCK : (j + 1) * BLOCK] = v

    unpack(packed_ref, nb, put)

    def body(b, carry):
        for bb in range(nb):
            lo, hi = bb * BLOCK, (bb + 1) * BLOCK

            @pl.when(b == bb)
            def _():
                d_ref[...] = s_ref[lo:hi, lo:hi]

        factor_block(d_ref, ud_ref, BLOCK // TILE)
        for bb in range(nb):
            lo, hi = bb * BLOCK, (bb + 1) * BLOCK

            @pl.when(b == bb)
            def _():
                u_ref[lo:hi, lo:hi] = ud_ref[...]
                if bb + 1 < nb:
                    u_ref[lo:hi, hi:] = dot(lower_part(d_ref[...]), s_ref[lo:hi, hi:])
                for ib in range(bb + 1, nb):
                    a = ib * BLOCK
                    s_ref[a : a + BLOCK, a:] = s_ref[a : a + BLOCK, a:] - dot(
                        u_ref[lo:hi, a : a + BLOCK], u_ref[lo:hi, a:], 0, 0
                    )

        return carry

    lax.fori_loop(0, nb, body, 0)
    y_ref[...] = dot(u_ref[...], x_ref[...], 0, 0)


def split(q):
    high = q.astype(jnp.bfloat16)
    low = (q - high.astype(F32)).astype(jnp.bfloat16)
    return high, low


def finish_kernel(
    info_ref, p0_ref, p1_ref, y_ref, values_hbm, out_ref, strengths_ref,
    g0_ref, g1_ref, d_ref, ud_ref, values_ref, sem,
):
    copy = pltpu.make_async_copy(values_hbm, values_ref, sem)
    copy.start()
    n, modes = y_ref.shape
    nb = n // BLOCK
    for packed, g in ((p0_ref, g0_ref), (p1_ref, g1_ref)):

        def put(i, j, h, v, g=g):
            r = i * BLOCK + h * 64
            g[r : r + 64, j * BLOCK : (j + 1) * BLOCK] = v
            if j > i:
                c = i * BLOCK + h * 64
                g[j * BLOCK : (j + 1) * BLOCK, c : c + 64] = v.T

        unpack(packed, nb, put)

    def normal(product):
        d_ref[...] = jnp.zeros_like(d_ref)
        d_ref[:, :modes] = product
        factor_block(d_ref, ud_ref, modes // TILE)
        return lower_part(d_ref[...])[:, :modes]

    y = y_ref[...]
    t = dot(g0_ref[...], y)
    inverse = normal(dot(y, t, 0, 0))
    q0 = dot(y, inverse, 1, 1)
    z = dot(t, inverse, 1, 1)
    w = dot(g1_ref[...], z)
    inverse = normal(dot(z, w, 0, 0))
    q1 = dot(z, inverse, 1, 1)
    row = lax.broadcasted_iota(jnp.int32, ud_ref.shape, 0)
    lane = lax.broadcasted_iota(jnp.int32, ud_ref.shape, 1)
    diagonal = jnp.where(row == lane, ud_ref[...], 0.0)
    strengths_ref[...] = jnp.sum(diagonal, axis=0, keepdims=True)
    q = jnp.where(info_ref[0] == 0, q0, q1)
    high, low = split(q)
    both = jnp.concatenate([high, low], axis=1)
    copy.wait()
    ocean = info_ref[1]
    rows = values_ref.shape[0]
    step = min(rows, 256)
    for r in range(0, rows, step):
        product = jnp.dot(values_ref[r : r + step, :], both, preferred_element_type=F32)
        total = product[:, :modes] + product[:, modes:]
        place = lax.broadcasted_iota(jnp.int32, total.shape, 0) + r
        out_ref[r : r + step, :] = jnp.where(place < ocean, total, 0.0)


def swap(value, axis, apart):
    return lax.ppermute(value, axis, [(i, i ^ 1 << apart) for i in range(lax.axis_size(axis))])


def has_bit(axis, apart):
    return (lax.axis_index(axis) >> apart) & 1 == 1


def sum_all(value):
    sizes = {axis: lax.axis_size(axis) for axis in ("row", "group")}
    if any(n & (n - 1) for n in sizes.values()):
        return lax.psum(value, ("group", "row"))
    bits = {axis: n.bit_length() - 1 for axis, n in sizes.items()}
    halved = [(axis, 0) for axis in ("row", "group") if bits[axis]]
    whole = [(axis, b) for axis in ("group", "row") for b in range(1, bits[axis])]
    for axis, b in halved:
        half = value.shape[0] // 2
        high = has_bit(axis, b)
        keep = jnp.where(high, value[half:], value[:half])
        send = jnp.where(high, value[:half], value[half:])
        value = keep + swap(send, axis, b)
    for axis, b in whole:
        value = value + swap(value, axis, b)
    for axis, b in reversed(halved):
        other = swap(value, axis, b)
        high = has_bit(axis, b)
        value = jnp.concatenate(
            [jnp.where(high, other, value), jnp.where(high, value, other)], axis=0
        )
    return value


def per_device(anomalies, valid_rows, start_basis):
    values = anomalies[0]
    rows_here, n = values.shape
    modes = start_basis.shape[1]
    nb = n // BLOCK
    ocean = valid_rows[0, 0]
    place = lax.broadcasted_iota(jnp.int32, (rows_here, 1), 0)
    masked = jnp.where(place < ocean, values, jnp.zeros_like(values))
    gram = lax.dot_general(
        masked, masked, (((0,), (0,)), ((), ())), preferred_element_type=F32
    )
    blocks = [
        gram[i * BLOCK : (i + 1) * BLOCK, j * BLOCK : (j + 1) * BLOCK] for i, j in pairs(nb)
    ]
    quarter = len(blocks) * BLOCK // 4
    packed = jnp.concatenate(blocks, axis=0).reshape(4, quarter, BLOCK)
    count = jnp.broadcast_to(ocean.astype(F32), (4, TILE, BLOCK))
    packed = jnp.concatenate([packed, count], axis=1)
    mine = sum_all(packed)
    other = swap(mine, "field", 0)
    which = lax.axis_index("field")
    p0 = jnp.where(which == 0, mine, other)
    p1 = jnp.where(which == 0, other, mine)
    y = pl.pallas_call(
        factor_kernel,
        out_shape=jax.ShapeDtypeStruct((n, modes), F32),
        in_specs=[VMEM, VMEM],
        out_specs=VMEM,
        scratch_shapes=[
            pltpu.VMEM((n, n), F32),
            pltpu.VMEM((n, n), F32),
            pltpu.VMEM((BLOCK, BLOCK), F32),
            pltpu.VMEM((BLOCK, BLOCK), F32),
        ],
    )(p1, start_basis)
    info = jnp.stack([which.astype(jnp.int32), ocean])
    patterns, strengths = pl.pallas_call(
        finish_kernel,
        out_shape=(
            jax.ShapeDtypeStruct((rows_here, modes), F32),
            jax.ShapeDtypeStruct((1, BLOCK), F32),
        ),
        in_specs=[SMEM, VMEM, VMEM, VMEM, pl.BlockSpec(memory_space=pl.ANY)],
        out_specs=(VMEM, VMEM),
        scratch_shapes=[
            pltpu.VMEM((n, n), F32),
            pltpu.VMEM((n, n), F32),
            pltpu.VMEM((modes, BLOCK), F32),
            pltpu.VMEM((modes, BLOCK), F32),
            pltpu.VMEM((rows_here, n), jnp.bfloat16),
            pltpu.SemaphoreType.DMA,
        ],
    )(info, p0, p1, y, values)
    return patterns[None], strengths[0, :modes]


def solution(mesh):
    in_specs = (P("field", ("group", "row"), None), P("field", ("group", "row")), P())
    out_specs = (P("field", ("group", "row"), None), P())
    return jax.shard_map(
        per_device, mesh=mesh, in_specs=in_specs, out_specs=out_specs, check_vma=False
    )
```

```python
import jax
import jax.numpy as jnp
from jax import lax
from jax.experimental import pallas as pl
from jax.experimental.pallas import tpu as pltpu
from jax.sharding import PartitionSpec as P

HIGH = lax.Precision.HIGHEST
F32 = jnp.float32
BLOCK = 128
TILE = 8
VMEM = pl.BlockSpec(memory_space=pltpu.VMEM)
SMEM = pl.BlockSpec(memory_space=pltpu.SMEM)


def dot(a, b, ca=1, cb=0):
    return lax.dot_general(
        a, b, (((ca,), (cb,)), ((), ())), precision=HIGH, preferred_element_type=F32
    )


def lane_copy(tile, lane):
    return jnp.broadcast_to(tile[:, lane : lane + 1], tile.shape)


def row_copy(tile, row):
    return jnp.broadcast_to(tile[row : row + 1, :], tile.shape)


def iotas(shape):
    return lax.broadcasted_iota(jnp.int32, shape, 0), lax.broadcasted_iota(jnp.int32, shape, 1)


def inverse_factor(tiles):
    tiles = list(tiles)
    steps = len(tiles)
    sub, lane = iotas((TILE, BLOCK))
    cols = [lane_copy(tiles[0], j) for j in range(TILE)]
    out = []
    for s in range(steps):
        k = TILE * s
        tile = tiles[s]
        inside = (lane >= k) & (lane < k + TILE)
        scale, low = [], {}
        for j in range(TILE):
            scale.append(lax.rsqrt(row_copy(cols[j], j)))
            column = cols[j] * scale[j]
            for i in range(j + 1, TILE):
                low[i, j] = row_copy(column, i)
            for c in range(j + 1, TILE):
                cols[c] = cols[c] - column * low[c, j]
        rows = []
        for i in range(TILE):
            row = jnp.where(inside, jnp.where(lane == k + i, 1.0, 0.0), row_copy(tile, i))
            for m in range(i):
                row = row - low[i, m] * rows[m]
            rows.append(row * scale[i])
        new = rows[0]
        for i in range(1, TILE):
            new = jnp.where(sub == i, rows[i], new)
        out.append(jnp.where(lane <= k + sub, new, 0.0))
        for g in range(s + 1, steps):
            t = tiles[g]
            w = []
            for j in range(TILE):
                acc = lane_copy(t, k + j)
                for m in range(j):
                    acc = acc - low[j, m] * w[m]
                w.append(acc * scale[j])
            if g == s + 1:
                cols = [lane_copy(t, k + TILE + c) for c in range(TILE)]
                for c in range(TILE):
                    for i in range(TILE):
                        cols[c] = cols[c] - w[i] * row_copy(w[i], c)
            t = jnp.where(inside, 0.0, t)
            for i in range(TILE):
                t = t - w[i] * rows[i]
            tiles[g] = t
    return out


def layout(nb):
    shared = [(i, i) for i in range(0, nb, 2)]
    return shared + [(i, j) for i in range(nb) for j in range(i + 1, nb)]


def pack(gram, count):
    nb = gram.shape[0] // BLOCK

    def block(i, j):
        return gram[i * BLOCK : (i + 1) * BLOCK, j * BLOCK : (j + 1) * BLOCK]

    row, lane = iotas((BLOCK, BLOCK))
    parts, extra = [], [jnp.full((1, BLOCK), count, F32)]
    for i, j in layout(nb):
        if i == j:
            second = block(i + 1, i + 1)
            parts.append(jnp.where(row <= lane, block(i, i), second))
            extra.append(jnp.sum(jnp.where(row == lane, second, 0.0), axis=0, keepdims=True))
        else:
            parts.append(block(i, j))
    fill = jnp.zeros((-len(extra) % TILE, BLOCK), F32)
    extra = jnp.concatenate(extra + [fill], axis=0)
    parts = jnp.concatenate(parts, axis=0)
    parts = parts.reshape(4, parts.shape[0] // 4, BLOCK)
    return jnp.concatenate([parts, jnp.broadcast_to(extra, (4,) + extra.shape)], axis=1)


def unpack(read, nb, put):
    quarter = nb * nb * BLOCK // 8
    row, lane = iotas((BLOCK, BLOCK))
    inverse = 1.0 / read(0, quarter, 1)

    def block(t):
        halves = []
        for start in (t * BLOCK, t * BLOCK + BLOCK // 2):
            part, offset = divmod(start, quarter)
            halves.append(read(part, offset, BLOCK // 2) * inverse)
        return jnp.concatenate(halves, axis=0)

    for t, (i, j) in enumerate(layout(nb)):
        if i == j:
            both = block(t)
            turned = both.T
            ends = read(0, quarter + 1 + i // 2, 1) * inverse
            put(i, i, jnp.where(row <= lane, both, turned))
            second = jnp.where(row > lane, both, turned)
            put(i + 1, i + 1, jnp.where(row == lane, ends, second))
        else:
            put(i, j, block(t))


def span(i):
    return slice(i * BLOCK, (i + 1) * BLOCK)


def factor_kernel(mine_ref, other_ref, x_ref, y_ref, s_ref, u_ref, d_ref):
    n = x_ref.shape[1]
    nb = n // BLOCK
    own = lax.axis_index("field") == 1

    def read(part, start, rows):
        a = mine_ref[part, start : start + rows, :]
        b = other_ref[part, start : start + rows, :]
        return jnp.where(own, a, b)

    def put(i, j, v):
        s_ref[span(i), span(j)] = v

    unpack(read, nb, put)
    row, lane = iotas((BLOCK, BLOCK))
    for b in range(nb):
        lo, hi = b * BLOCK, (b + 1) * BLOCK
        tiles = [s_ref[lo + r : lo + r + TILE, lo:hi] for r in range(0, BLOCK, TILE)]
        for t, tile in enumerate(inverse_factor(tiles)):
            d_ref[TILE * t : TILE * (t + 1), :] = tile
        u_ref[:, lo:] = dot(d_ref[...], s_ref[lo:hi, lo:])
        for i in range(b + 1, nb):
            a = i * BLOCK
            s_ref[span(i), a:] = s_ref[span(i), a:] - dot(u_ref[:, span(i)], u_ref[:, a:], 0, 0)
        product = dot(x_ref[:, lo:hi], u_ref[:, lo:])
        y_ref[:, lo:] = product if b == 0 else y_ref[:, lo:] + product


def finish_kernel(
    valid_ref, mine_ref, other_ref, y_ref, values_hbm, out_ref, strengths_ref,
    g_ref, values_ref, sem,
):
    copy = pltpu.make_async_copy(values_hbm, values_ref, sem)
    copy.start()
    modes, n = y_ref.shape
    nb = n // BLOCK
    first = lax.axis_index("field") == 0
    for f in range(2):

        def read(part, start, rows, f=f):
            a = mine_ref[part, start : start + rows, :]
            b = other_ref[part, start : start + rows, :]
            return jnp.where(first, a, b) if f == 0 else jnp.where(first, b, a)

        def put(i, j, v, f=f):
            g_ref[f, span(i), span(j)] = v
            if i != j:
                g_ref[f, span(j), span(i)] = v.T

        unpack(read, nb, put)

    def normal(product):
        wide = jnp.concatenate([product, jnp.zeros((modes, BLOCK - modes), F32)], axis=1)
        tiles = [wide[r : r + TILE, :] for r in range(0, modes, TILE)]
        return jnp.concatenate(inverse_factor(tiles), axis=0)[:, :modes]

    y = y_ref[...]
    t = dot(y, g_ref[0])
    inverse = normal(dot(y, t, 1, 1))
    q0 = dot(inverse, y)
    z = dot(inverse, t)
    w = dot(z, g_ref[1])
    inverse = normal(dot(z, w, 1, 1))
    q1 = dot(inverse, z)
    row, lane = iotas((modes, modes))
    diagonal = jnp.sum(jnp.where(row == lane, inverse, 0.0), axis=0, keepdims=True)
    strengths_ref[...] = 1.0 / diagonal
    q = jnp.where(first, q0, q1)
    high = q.astype(jnp.bfloat16)
    low = (q - high.astype(F32)).astype(jnp.bfloat16)
    both = jnp.concatenate([high, low], axis=0)
    copy.wait()
    ocean = valid_ref[0, 0]
    points = values_ref.shape[0]
    step = min(points, 256)
    for r in range(0, points, step):
        product = lax.dot_general(
            both, values_ref[r : r + step, :], (((1,), (1,)), ((), ())),
            preferred_element_type=F32,
        )
        total = product[:modes] + product[modes:]
        _, place = iotas(total.shape)
        out_ref[:, r : r + step] = jnp.where(place + r < ocean, total, 0.0)


AXES = ("field", "group", "row")


def swap(value, which):
    sizes = [lax.axis_size(a) for a in AXES]
    moves = []
    for f in range(sizes[0]):
        axis, b = which(f)
        for g in range(sizes[1]):
            for r in range(sizes[2]):
                there = dict(zip(AXES, (f, g, r)))
                there[axis] ^= 1 << b
                here = (f * sizes[1] + g) * sizes[2] + r
                moves.append(
                    (here, (there["field"] * sizes[1] + there["group"]) * sizes[2] + there["row"])
                )
    return lax.ppermute(value, AXES, moves)


def has_bit(which):
    def of(f):
        axis, b = which(f)
        return (lax.axis_index(axis) >> b) & 1 == 1

    return jnp.where(lax.axis_index("field") == 0, of(0), of(1))


def sum_all(value):
    sizes = {axis: lax.axis_size(axis) for axis in ("row", "group")}
    if any(n & (n - 1) for n in sizes.values()) or min(sizes.values()) < 2:
        return lax.psum(value, ("group", "row"))
    bits = {axis: n.bit_length() - 1 for axis, n in sizes.items()}
    halved = [("row", 0), ("group", 0)]
    whole = [(axis, b) for axis in ("group", "row") for b in range(1, bits[axis])]
    orders = [lambda f, k=k: halved[k ^ f] for k in range(2)]
    turned = whole[1:] + whole[:1]
    for which in orders:
        half = value.shape[0] // 2
        high = has_bit(which)
        keep = jnp.where(high, value[half:], value[:half])
        send = jnp.where(high, value[:half], value[half:])
        value = keep + swap(send, which)
    for pair in zip(whole, turned):
        value = value + swap(value, lambda f, pair=pair: pair[f])
    for which in reversed(orders):
        other = swap(value, which)
        high = has_bit(which)
        value = jnp.concatenate(
            [jnp.where(high, other, value), jnp.where(high, value, other)], axis=0
        )
    return value


def per_device(anomalies, valid_rows, start_basis):
    values = anomalies[0]
    rows_here, n = values.shape
    modes = start_basis.shape[1]
    ocean = valid_rows[0, 0]
    place = lax.broadcasted_iota(jnp.int32, (rows_here, 1), 0)
    masked = jnp.where(place < ocean, values, jnp.zeros_like(values))
    gram = lax.dot_general(
        masked, masked, (((0,), (0,)), ((), ())), preferred_element_type=F32
    )
    mine = sum_all(pack(gram, ocean.astype(F32)))
    other = swap(mine, lambda f: ("field", 0))
    y = pl.pallas_call(
        factor_kernel,
        out_shape=jax.ShapeDtypeStruct((modes, n), F32),
        in_specs=[VMEM, VMEM, VMEM],
        out_specs=VMEM,
        scratch_shapes=[
            pltpu.VMEM((n, n), F32),
            pltpu.VMEM((BLOCK, n), F32),
            pltpu.VMEM((BLOCK, BLOCK), F32),
        ],
    )(mine, other, start_basis.T)
    patterns, strengths = pl.pallas_call(
        finish_kernel,
        out_shape=(
            jax.ShapeDtypeStruct((modes, rows_here), F32),
            jax.ShapeDtypeStruct((1, modes), F32),
        ),
        in_specs=[SMEM, VMEM, VMEM, VMEM, pl.BlockSpec(memory_space=pl.ANY)],
        out_specs=(VMEM, VMEM),
        scratch_shapes=[
            pltpu.VMEM((2, n, n), F32),
            pltpu.VMEM((rows_here, n), jnp.bfloat16),
            pltpu.SemaphoreType.DMA,
        ],
    )(valid_rows, mine, other, y, values)
    return patterns.T[None], strengths[0]


def solution(mesh):
    in_specs = (P("field", ("group", "row"), None), P("field", ("group", "row")), P())
    out_specs = (P("field", ("group", "row"), None), P())
    return jax.shard_map(
        per_device, mesh=mesh, in_specs=in_specs, out_specs=out_specs, check_vma=False
    )
```

```python
import jax
import jax.numpy as jnp
from jax import lax
from jax.experimental import pallas as pl
from jax.experimental.pallas import tpu as pltpu
from jax.sharding import PartitionSpec as P

HIGH = lax.Precision.HIGHEST
F32 = jnp.float32
BLOCK = 128
TILE = 8
GRANT = 16 * 2**20
VMEM = pl.BlockSpec(memory_space=pltpu.VMEM)
SMEM = pl.BlockSpec(memory_space=pltpu.SMEM)


def dot(a, b, ca=1, cb=0):
    return lax.dot_general(
        a, b, (((ca,), (cb,)), ((), ())), precision=HIGH, preferred_element_type=F32
    )


def lane_copy(tile, lane):
    return jnp.broadcast_to(tile[:, lane : lane + 1], tile.shape)


def row_copy(tile, row):
    return jnp.broadcast_to(tile[row : row + 1, :], tile.shape)


def iotas(shape):
    return lax.broadcasted_iota(jnp.int32, shape, 0), lax.broadcasted_iota(jnp.int32, shape, 1)


def inverse_factor(tiles):
    tiles = list(tiles)
    steps = len(tiles)
    sub, lane = iotas((TILE, BLOCK))
    cols = [lane_copy(tiles[0], j) for j in range(TILE)]
    out = []
    for s in range(steps):
        k = TILE * s
        tile = tiles[s]
        inside = (lane >= k) & (lane < k + TILE)
        scale, low = [], {}
        for j in range(TILE):
            scale.append(lax.rsqrt(row_copy(cols[j], j)))
            column = cols[j] * scale[j]
            for i in range(j + 1, TILE):
                low[i, j] = row_copy(column, i)
            for c in range(j + 1, TILE):
                cols[c] = cols[c] - column * low[c, j]
        rows = []
        for i in range(TILE):
            row = jnp.where(inside, jnp.where(lane == k + i, 1.0, 0.0), row_copy(tile, i))
            for m in range(i):
                row = row - low[i, m] * rows[m]
            rows.append(row * scale[i])
        new = rows[0]
        for i in range(1, TILE):
            new = jnp.where(sub == i, rows[i], new)
        out.append(jnp.where(lane <= k + sub, new, 0.0))
        for g in range(s + 1, steps):
            t = tiles[g]
            w = []
            for j in range(TILE):
                acc = lane_copy(t, k + j)
                for m in range(j):
                    acc = acc - low[j, m] * w[m]
                w.append(acc * scale[j])
            if g == s + 1:
                cols = [lane_copy(t, k + TILE + c) for c in range(TILE)]
                for c in range(TILE):
                    for i in range(TILE):
                        cols[c] = cols[c] - w[i] * row_copy(w[i], c)
            t = jnp.where(inside, 0.0, t)
            for i in range(TILE):
                t = t - w[i] * rows[i]
            tiles[g] = t
    return out


def layout(nb):
    shared = [(i, i) for i in range(0, nb, 2)]
    return shared + [(i, j) for i in range(nb) for j in range(i + 1, nb)]


def pack(gram, count):
    nb = gram.shape[0] // BLOCK

    def block(i, j):
        return gram[i * BLOCK : (i + 1) * BLOCK, j * BLOCK : (j + 1) * BLOCK]

    row, lane = iotas((BLOCK, BLOCK))
    parts, extra = [], [jnp.full((1, BLOCK), count, F32)]
    for i, j in layout(nb):
        if i == j:
            second = block(i + 1, i + 1)
            parts.append(jnp.where(row <= lane, block(i, i), second))
            extra.append(jnp.sum(jnp.where(row == lane, second, 0.0), axis=0, keepdims=True))
        else:
            parts.append(block(i, j))
    fill = jnp.zeros((-len(extra) % TILE, BLOCK), F32)
    extra = jnp.concatenate(extra + [fill], axis=0)
    parts = jnp.concatenate(parts, axis=0)
    parts = parts.reshape(4, parts.shape[0] // 4, BLOCK)
    return jnp.concatenate([parts, jnp.broadcast_to(extra, (4,) + extra.shape)], axis=1)


def unpack(read, nb, put):
    quarter = nb * nb * BLOCK // 8
    row, lane = iotas((BLOCK, BLOCK))
    inverse = 1.0 / read(0, quarter, 1)

    def block(t):
        halves = []
        for start in (t * BLOCK, t * BLOCK + BLOCK // 2):
            part, offset = divmod(start, quarter)
            halves.append(read(part, offset, BLOCK // 2) * inverse)
        return jnp.concatenate(halves, axis=0)

    for t, (i, j) in enumerate(layout(nb)):
        if i == j:
            both = block(t)
            turned = both.T
            ends = read(0, quarter + 1 + i // 2, 1) * inverse
            put(i, i, jnp.where(row <= lane, both, turned))
            second = jnp.where(row > lane, both, turned)
            put(i + 1, i + 1, jnp.where(row == lane, ends, second))
        else:
            put(i, j, block(t))


def span(i):
    return slice(i * BLOCK, (i + 1) * BLOCK)


def factor_kernel(part_ref, rest_ref, x_ref, y_ref, s_ref, u_ref, d_ref):
    @pl.when(lax.axis_index("field") == 0)
    def _():
        y_ref[...] = jnp.zeros_like(y_ref)

    @pl.when(lax.axis_index("field") == 1)
    def _():
        apply_factor(part_ref, rest_ref, x_ref, y_ref, s_ref, u_ref, d_ref)


def apply_factor(part_ref, rest_ref, x_ref, y_ref, s_ref, u_ref, d_ref):
    n = x_ref.shape[1]
    nb = n // BLOCK
    half = part_ref.shape[0]
    high = has_bit(bit_orders()[0])

    def read(part, start, rows):
        a = part_ref[part % half, start : start + rows, :]
        b = rest_ref[part % half, start : start + rows, :]
        return jnp.where(high, a, b) if part >= half else jnp.where(high, b, a)

    def put(i, j, v):
        s_ref[span(i), span(j)] = v

    unpack(read, nb, put)
    for b in range(nb):
        lo, hi = b * BLOCK, (b + 1) * BLOCK
        tiles = [s_ref[lo + r : lo + r + TILE, lo:hi] for r in range(0, BLOCK, TILE)]
        for t, tile in enumerate(inverse_factor(tiles)):
            d_ref[TILE * t : TILE * (t + 1), :] = tile
        u_ref[:, lo:] = dot(d_ref[...], s_ref[lo:hi, lo:])
        for i in range(b + 1, nb):
            a = i * BLOCK
            s_ref[span(i), a:] = s_ref[span(i), a:] - dot(u_ref[:, span(i)], u_ref[:, a:], 0, 0)
        product = dot(x_ref[:, lo:hi], u_ref[:, lo:])
        y_ref[:, lo:] = product if b == 0 else y_ref[:, lo:] + product


def finish_kernel(
    valid_ref, mine_ref, other_ref, y_ref, y_other_ref, values_hbm, out_ref, strengths_ref,
    g_ref, values_ref, sem,
):
    copy = pltpu.make_async_copy(values_hbm, values_ref, sem)
    copy.start()
    modes, n = y_ref.shape
    nb = n // BLOCK
    first = lax.axis_index("field") == 0
    for f in range(2):

        def read(part, start, rows, f=f):
            a = mine_ref[part, start : start + rows, :]
            b = other_ref[part, start : start + rows, :]
            return jnp.where(first, a, b) if f == 0 else jnp.where(first, b, a)

        def put(i, j, v, f=f):
            g_ref[f, span(i), span(j)] = v
            if i != j:
                g_ref[f, span(j), span(i)] = v.T

        unpack(read, nb, put)

    def normal(product):
        wide = jnp.concatenate([product, jnp.zeros((modes, BLOCK - modes), F32)], axis=1)
        tiles = [wide[r : r + TILE, :] for r in range(0, modes, TILE)]
        return jnp.concatenate(inverse_factor(tiles), axis=0)[:, :modes]

    y = jnp.where(first, y_other_ref[...], y_ref[...])
    t = dot(y, g_ref[0])
    inverse = normal(dot(y, t, 1, 1))
    q0 = dot(inverse, y)
    z = dot(inverse, t)
    w = dot(z, g_ref[1])
    inverse = normal(dot(z, w, 1, 1))
    q1 = dot(inverse, z)
    row, lane = iotas((modes, modes))
    diagonal = jnp.sum(jnp.where(row == lane, inverse, 0.0), axis=0, keepdims=True)
    strengths_ref[...] = 1.0 / diagonal
    q = jnp.where(first, q0, q1)
    high = q.astype(jnp.bfloat16)
    low = (q - high.astype(F32)).astype(jnp.bfloat16)
    both = jnp.concatenate([high, low], axis=0)
    copy.wait()
    ocean = valid_ref[0, 0]
    points = values_ref.shape[0]
    step = min(points, 256)
    for r in range(0, points, step):
        product = lax.dot_general(
            both, values_ref[r : r + step, :], (((1,), (1,)), ((), ())),
            preferred_element_type=F32,
        )
        total = product[:modes] + product[modes:]
        _, place = iotas(total.shape)
        out_ref[:, r : r + step] = jnp.where(place + r < ocean, total, 0.0)


AXES = ("field", "group", "row")


def swap(value, which):
    sizes = [lax.axis_size(a) for a in AXES]
    moves = []
    for f in range(sizes[0]):
        axis, b = which(f)
        for g in range(sizes[1]):
            for r in range(sizes[2]):
                there = dict(zip(AXES, (f, g, r)))
                there[axis] ^= 1 << b
                here = (f * sizes[1] + g) * sizes[2] + r
                moves.append(
                    (here, (there["field"] * sizes[1] + there["group"]) * sizes[2] + there["row"])
                )
    return lax.ppermute(value, AXES, moves)


def has_bit(which):
    def of(f):
        axis, b = which(f)
        return (lax.axis_index(axis) >> b) & 1 == 1

    return jnp.where(lax.axis_index("field") == 0, of(0), of(1))


def bit_orders():
    sizes = {axis: lax.axis_size(axis) for axis in ("row", "group")}
    bits = {axis: n.bit_length() - 1 for axis, n in sizes.items()}
    order = [("row", 0), ("group", 0)]
    order += [(axis, b) for axis in ("row", "group") for b in range(1, bits[axis])]
    return [lambda f, k=k: order[(k + 2 * (1 - f)) % len(order)] for k in range(len(order))]


def joined(high, value, other):
    return jnp.concatenate(
        [jnp.where(high, other, value), jnp.where(high, value, other)], axis=0
    )


def sum_all(value):
    orders = bit_orders()
    for which in orders[:2]:
        half = value.shape[0] // 2
        high = has_bit(which)
        keep = jnp.where(high, value[half:], value[:half])
        send = jnp.where(high, value[:half], value[half:])
        value = keep + swap(send, which)
    for which in orders[2:]:
        value = value + swap(value, which)
    value = joined(has_bit(orders[1]), value, swap(value, orders[1]))
    return value, swap(value, orders[0])


def per_device(anomalies, valid_rows, start_basis):
    values = anomalies[0]
    rows_here, n = values.shape
    modes = start_basis.shape[1]
    ocean = valid_rows[0, 0]
    place = lax.broadcasted_iota(jnp.int32, (rows_here, 1), 0)
    masked = jnp.where(place < ocean, values, jnp.zeros_like(values))
    gram = lax.dot_general(
        masked, masked, (((0,), (0,)), ((), ())), preferred_element_type=F32
    )
    part, rest = sum_all(pack(gram, ocean.astype(F32)))
    mine = joined(has_bit(bit_orders()[0]), part, rest)
    y = pl.pallas_call(
        factor_kernel,
        out_shape=jax.ShapeDtypeStruct((modes, n), F32),
        in_specs=[VMEM, VMEM, VMEM],
        out_specs=VMEM,
        scratch_shapes=[
            pltpu.VMEM((n, n), F32),
            pltpu.VMEM((BLOCK, n), F32),
            pltpu.VMEM((BLOCK, BLOCK), F32),
        ],
        compiler_params=pltpu.CompilerParams(vmem_limit_bytes=GRANT),
    )(part, rest, start_basis.T)
    y, mine = lax.optimization_barrier((y, mine))
    partner = lambda f: ("field", 0)
    y_other = swap(y, partner)
    other = swap(mine, partner)
    patterns, strengths = pl.pallas_call(
        finish_kernel,
        out_shape=(
            jax.ShapeDtypeStruct((modes, rows_here), F32),
            jax.ShapeDtypeStruct((1, modes), F32),
        ),
        in_specs=[SMEM, VMEM, VMEM, VMEM, VMEM, pl.BlockSpec(memory_space=pl.ANY)],
        out_specs=(VMEM, VMEM),
        scratch_shapes=[
            pltpu.VMEM((2, n, n), F32),
            pltpu.VMEM((rows_here, n), jnp.bfloat16),
            pltpu.SemaphoreType.DMA,
        ],
        compiler_params=pltpu.CompilerParams(vmem_limit_bytes=GRANT),
    )(valid_rows, mine, other, y, y_other, values)
    return patterns.T[None], strengths[0]


def solution(mesh):
    in_specs = (P("field", ("group", "row"), None), P("field", ("group", "row")), P())
    out_specs = (P("field", ("group", "row"), None), P())
    return jax.shard_map(
        per_device, mesh=mesh, in_specs=in_specs, out_specs=out_specs, check_vma=False
    )
```

```python
import jax
import jax.numpy as jnp
from jax import lax
from jax.experimental import pallas as pl
from jax.experimental.pallas import tpu as pltpu
from jax.sharding import PartitionSpec as P

HIGH = lax.Precision.HIGHEST
F32 = jnp.float32
BLOCK = 128
TILE = 8
HALF = 64
GRANT = 16 * 2**20
VMEM = pl.BlockSpec(memory_space=pltpu.VMEM)
SMEM = pl.BlockSpec(memory_space=pltpu.SMEM)


def dot(a, b, ca=1, cb=0):
    return lax.dot_general(
        a, b, (((ca,), (cb,)), ((), ())), precision=HIGH, preferred_element_type=F32
    )


def thirds(x):
    high = x.astype(jnp.bfloat16)
    rest = x - high.astype(F32)
    middle = rest.astype(jnp.bfloat16)
    return high, middle, (rest - middle.astype(F32)).astype(jnp.bfloat16)


def stacked(a, b, dim=0):
    ah, am, al = thirds(a)
    bh, bm, bl = thirds(b)
    return lax.dot_general(
        jnp.concatenate([ah, ah, am, ah, al, am], axis=dim),
        jnp.concatenate([bh, bm, bh, bl, bh, bm], axis=0),
        (((dim,), (0,)), ((), ())),
        preferred_element_type=F32,
    )


def lane_copy(tile, lane):
    return jnp.broadcast_to(tile[:, lane : lane + 1], tile.shape)


def row_copy(tile, row):
    return jnp.broadcast_to(tile[row : row + 1, :], tile.shape)


def iotas(shape):
    return lax.broadcasted_iota(jnp.int32, shape, 0), lax.broadcasted_iota(jnp.int32, shape, 1)


def eliminate(tiles, base):
    tiles = list(tiles)
    steps = len(tiles)
    sub, lane = iotas((TILE, BLOCK))
    cols = [lane_copy(tiles[0], base + j) for j in range(TILE)]
    out = []
    for s in range(steps):
        k = base + TILE * s
        tile = tiles[s]
        inside = (lane >= k) & (lane < k + TILE)
        scale, low = [], {}
        for j in range(TILE):
            scale.append(lax.rsqrt(row_copy(cols[j], j)))
            column = cols[j] * scale[j]
            for i in range(j + 1, TILE):
                low[i, j] = row_copy(column, i)
            for c in range(j + 1, TILE):
                cols[c] = cols[c] - column * low[c, j]
        rows = []
        for i in range(TILE):
            row = jnp.where(inside, jnp.where(lane == k + i, 1.0, 0.0), row_copy(tile, i))
            for m in range(i):
                row = row - low[i, m] * rows[m]
            rows.append(row * scale[i])
        new = rows[0]
        for i in range(1, TILE):
            new = jnp.where(sub == i, rows[i], new)
        out.append(new)
        for g in range(s + 1, steps):
            t = tiles[g]
            w = []
            for j in range(TILE):
                acc = lane_copy(t, k + j)
                for m in range(j):
                    acc = acc - low[j, m] * w[m]
                w.append(acc * scale[j])
            if g == s + 1:
                cols = [lane_copy(t, k + TILE + c) for c in range(TILE)]
                for c in range(TILE):
                    for i in range(TILE):
                        cols[c] = cols[c] - w[i] * row_copy(w[i], c)
            t = jnp.where(inside, 0.0, t)
            for i in range(TILE):
                t = t - w[i] * rows[i]
            tiles[g] = t
    return out


def inverse_factor(tiles, size):
    tiles = list(tiles)
    out = []
    count = size // TILE
    _, lane = iotas((TILE, BLOCK))
    for base in range(0, len(tiles) * TILE, size):
        done = eliminate(tiles[:count], base)
        out += done
        tiles = tiles[count:]
        if tiles:
            rows = jnp.concatenate(done, axis=0)
            place, at = iotas(rows.shape)
            keep = (at <= place + base) | (at >= base + size)
            update = stacked(rows, jnp.where(keep, rows, 0.0))
            for g in range(len(tiles)):
                start = base + size + TILE * g
                kept = jnp.where(lane < base + size, jnp.where(lane < base, tiles[g], 0.0), tiles[g])
                tiles[g] = kept - update[start : start + TILE, :]
    sub, _ = iotas((TILE, BLOCK))
    return [jnp.where(lane <= TILE * s + sub, t, 0.0) for s, t in enumerate(out)]


def layout(nb):
    shared = [(i, i) for i in range(0, nb, 2)]
    return shared + [(i, j) for i in range(nb) for j in range(i + 1, nb)]


def pack(gram, count):
    nb = gram.shape[0] // BLOCK

    def block(i, j):
        return gram[i * BLOCK : (i + 1) * BLOCK, j * BLOCK : (j + 1) * BLOCK]

    row, lane = iotas((BLOCK, BLOCK))
    parts, extra = [], [jnp.full((1, BLOCK), count, F32)]
    for i, j in layout(nb):
        if i == j:
            second = block(i + 1, i + 1)
            parts.append(jnp.where(row <= lane, block(i, i), second))
            extra.append(jnp.sum(jnp.where(row == lane, second, 0.0), axis=0, keepdims=True))
        else:
            parts.append(block(i, j))
    fill = jnp.zeros((-len(extra) % TILE, BLOCK), F32)
    extra = jnp.concatenate(extra + [fill], axis=0)
    parts = jnp.concatenate(parts, axis=0)
    parts = parts.reshape(4, parts.shape[0] // 4, BLOCK)
    return jnp.concatenate([parts, jnp.broadcast_to(extra, (4,) + extra.shape)], axis=1)


def unpack(read, nb, put):
    quarter = nb * nb * BLOCK // 8
    row, lane = iotas((BLOCK, BLOCK))
    inverse = 1.0 / read(0, quarter, 1)

    def block(t):
        halves = []
        for start in (t * BLOCK, t * BLOCK + BLOCK // 2):
            part, offset = divmod(start, quarter)
            halves.append(read(part, offset, BLOCK // 2) * inverse)
        return jnp.concatenate(halves, axis=0)

    for t, (i, j) in enumerate(layout(nb)):
        if i == j:
            both = block(t)
            turned = both.T
            ends = read(0, quarter + 1 + i // 2, 1) * inverse
            put(i, i, jnp.where(row <= lane, both, turned))
            second = jnp.where(row > lane, both, turned)
            put(i + 1, i + 1, jnp.where(row == lane, ends, second))
        else:
            put(i, j, block(t))


def span(i):
    return slice(i * BLOCK, (i + 1) * BLOCK)


def factor_kernel(part_ref, rest_ref, x_hbm, y_ref, s_ref, u_ref, x_ref, sem):
    @pl.when(lax.axis_index("field") == 0)
    def _():
        y_ref[...] = jnp.zeros_like(y_ref)

    @pl.when(lax.axis_index("field") == 1)
    def _():
        apply_factor(part_ref, rest_ref, x_hbm, y_ref, s_ref, u_ref, x_ref, sem)


def apply_factor(part_ref, rest_ref, x_hbm, y_ref, s_ref, u_ref, x_ref, sem):
    copy = pltpu.make_async_copy(x_hbm, x_ref, sem)
    copy.start()
    n = x_ref.shape[1]
    nb = n // BLOCK
    half = part_ref.shape[0]
    high = has_bit(bit_orders()[0])

    def read(part, start, rows):
        a = part_ref[part % half, start : start + rows, :]
        b = rest_ref[part % half, start : start + rows, :]
        return jnp.where(high, a, b) if part >= half else jnp.where(high, b, a)

    def put(i, j, v):
        s_ref[span(i), span(j)] = v

    unpack(read, nb, put)
    for b in range(nb):
        lo, hi = b * BLOCK, (b + 1) * BLOCK
        tiles = [s_ref[lo + r : lo + r + TILE, lo:hi] for r in range(0, BLOCK, TILE)]
        inverse = jnp.concatenate(inverse_factor(tiles, HALF), axis=0)
        if hi < n:
            near = stacked(inverse, s_ref[lo:hi, hi : hi + BLOCK], 1)
            u_ref[:, hi : hi + BLOCK] = near
            s_ref[span(b + 1), hi : hi + BLOCK] -= stacked(near, near)
        if hi + BLOCK < n:
            u_ref[:, hi + BLOCK :] = stacked(inverse, s_ref[lo:hi, hi + BLOCK :], 1)
            s_ref[span(b + 1), hi + BLOCK :] -= stacked(near, u_ref[:, hi + BLOCK :])
        u_ref[:, lo:hi] = stacked(inverse, s_ref[lo:hi, lo:hi], 1)
        for i in range(b + 2, nb):
            s_ref[span(i), i * BLOCK :] -= stacked(u_ref[:, span(i)], u_ref[:, i * BLOCK :])
        if b == 0:
            copy.wait()
        product = dot(x_ref[:, lo:hi], u_ref[:, lo:])
        y_ref[:, lo:] = product if b == 0 else y_ref[:, lo:] + product


def finish_kernel(
    valid_ref, mine_ref, other_ref, y_ref, y_other_ref, values_hbm, out_ref, strengths_ref,
    g_ref, values_ref, sem,
):
    copy = pltpu.make_async_copy(values_hbm, values_ref, sem)
    copy.start()
    modes, n = y_ref.shape
    nb = n // BLOCK
    first = lax.axis_index("field") == 0
    for f in range(2):

        def read(part, start, rows, f=f):
            a = mine_ref[part, start : start + rows, :]
            b = other_ref[part, start : start + rows, :]
            return jnp.where(first, a, b) if f == 0 else jnp.where(first, b, a)

        def put(i, j, v, f=f):
            g_ref[f, span(i), span(j)] = v
            if i != j:
                g_ref[f, span(j), span(i)] = v.T

        unpack(read, nb, put)

    def normal(product):
        wide = jnp.concatenate([product, jnp.zeros((modes, BLOCK - modes), F32)], axis=1)
        tiles = [wide[r : r + TILE, :] for r in range(0, modes, TILE)]
        return jnp.concatenate(inverse_factor(tiles, modes), axis=0)[:, :modes]

    y = jnp.where(first, y_other_ref[...], y_ref[...])
    t = dot(y, g_ref[0])
    inverse = normal(dot(y, t, 1, 1))
    q0 = dot(inverse, y)
    z = dot(inverse, t)
    w = dot(z, g_ref[1])
    inverse = normal(dot(z, w, 1, 1))
    q1 = dot(inverse, z)
    row, lane = iotas((modes, modes))
    diagonal = jnp.sum(jnp.where(row == lane, inverse, 0.0), axis=0, keepdims=True)
    strengths_ref[...] = 1.0 / diagonal
    q = jnp.where(first, q0, q1)
    high = q.astype(jnp.bfloat16)
    low = (q - high.astype(F32)).astype(jnp.bfloat16)
    both = jnp.concatenate([high, low], axis=0)
    copy.wait()
    ocean = valid_ref[0, 0]
    points = values_ref.shape[0]
    step = min(points, 256)
    for r in range(0, points, step):
        product = lax.dot_general(
            both, values_ref[r : r + step, :], (((1,), (1,)), ((), ())),
            preferred_element_type=F32,
        )
        total = product[:modes] + product[modes:]
        _, place = iotas(total.shape)
        out_ref[:, r : r + step] = jnp.where(place + r < ocean, total, 0.0)


AXES = ("field", "group", "row")


def swap(value, which):
    sizes = [lax.axis_size(a) for a in AXES]
    moves = []
    for f in range(sizes[0]):
        axis, b = which(f)
        for g in range(sizes[1]):
            for r in range(sizes[2]):
                there = dict(zip(AXES, (f, g, r)))
                there[axis] ^= 1 << b
                here = (f * sizes[1] + g) * sizes[2] + r
                moves.append(
                    (here, (there["field"] * sizes[1] + there["group"]) * sizes[2] + there["row"])
                )
    return lax.ppermute(value, AXES, moves)


def has_bit(which):
    def of(f):
        axis, b = which(f)
        return (lax.axis_index(axis) >> b) & 1 == 1

    return jnp.where(lax.axis_index("field") == 0, of(0), of(1))


def bit_orders():
    sizes = {axis: lax.axis_size(axis) for axis in ("row", "group")}
    bits = {axis: n.bit_length() - 1 for axis, n in sizes.items()}
    order = [("row", 0), ("group", 0)]
    order += [(axis, b) for axis in ("row", "group") for b in range(1, bits[axis])]
    return [lambda f, k=k: order[(k + 2 * (1 - f)) % len(order)] for k in range(len(order))]


def joined(high, value, other):
    return jnp.concatenate(
        [jnp.where(high, other, value), jnp.where(high, value, other)], axis=0
    )


def sum_all(value):
    orders = bit_orders()
    for which in orders[:2]:
        half = value.shape[0] // 2
        high = has_bit(which)
        keep = jnp.where(high, value[half:], value[:half])
        send = jnp.where(high, value[:half], value[half:])
        value = keep + swap(send, which)
    for which in orders[2:]:
        value = value + swap(value, which)
    value = joined(has_bit(orders[1]), value, swap(value, orders[1]))
    return value, swap(value, orders[0])


def per_device(anomalies, valid_rows, start_basis):
    values = anomalies[0]
    rows_here, n = values.shape
    modes = start_basis.shape[1]
    ocean = valid_rows[0, 0]
    place = lax.broadcasted_iota(jnp.int32, (rows_here, 1), 0)
    masked = jnp.where(place < ocean, values, jnp.zeros_like(values))
    gram = lax.dot_general(
        masked, masked, (((0,), (0,)), ((), ())), preferred_element_type=F32
    )
    part, rest = sum_all(pack(gram, ocean.astype(F32)))
    mine = joined(has_bit(bit_orders()[0]), part, rest)
    y = pl.pallas_call(
        factor_kernel,
        out_shape=jax.ShapeDtypeStruct((modes, n), F32),
        in_specs=[VMEM, VMEM, pl.BlockSpec(memory_space=pltpu.HBM)],
        out_specs=VMEM,
        scratch_shapes=[
            pltpu.VMEM((n, n), F32),
            pltpu.VMEM((BLOCK, n), F32),
            pltpu.VMEM((modes, n), F32),
            pltpu.SemaphoreType.DMA,
        ],
        compiler_params=pltpu.CompilerParams(vmem_limit_bytes=GRANT),
    )(part, rest, start_basis.T)
    y, mine = lax.optimization_barrier((y, mine))
    partner = lambda f: ("field", 0)
    y_other = swap(y, partner)
    other = swap(mine, partner)
    patterns, strengths = pl.pallas_call(
        finish_kernel,
        out_shape=(
            jax.ShapeDtypeStruct((modes, rows_here), F32),
            jax.ShapeDtypeStruct((1, modes), F32),
        ),
        in_specs=[SMEM, VMEM, VMEM, VMEM, VMEM, pl.BlockSpec(memory_space=pl.ANY)],
        out_specs=(VMEM, VMEM),
        scratch_shapes=[
            pltpu.VMEM((2, n, n), F32),
            pltpu.VMEM((rows_here, n), jnp.bfloat16),
            pltpu.SemaphoreType.DMA,
        ],
        compiler_params=pltpu.CompilerParams(vmem_limit_bytes=GRANT),
    )(valid_rows, mine, other, y, y_other, values)
    return patterns.T[None], strengths[0]


def solution(mesh):
    in_specs = (P("field", ("group", "row"), None), P("field", ("group", "row")), P())
    out_specs = (P("field", ("group", "row"), None), P())
    return jax.shard_map(
        per_device, mesh=mesh, in_specs=in_specs, out_specs=out_specs, check_vma=False
    )
```

```python
import jax
import jax.numpy as jnp
from jax import lax
from jax.experimental import pallas as pl
from jax.experimental.pallas import tpu as pltpu
from jax.sharding import PartitionSpec as P

HIGH = lax.Precision.HIGHEST
F32 = jnp.float32
BLOCK = 128
TILE = 8
HALF = 64
GRANT = 16 * 2**20
VMEM = pl.BlockSpec(memory_space=pltpu.VMEM)
SMEM = pl.BlockSpec(memory_space=pltpu.SMEM)


def dot(a, b, ca=1, cb=0):
    return lax.dot_general(
        a, b, (((ca,), (cb,)), ((), ())), precision=HIGH, preferred_element_type=F32
    )


def thirds(x):
    high = x.astype(jnp.bfloat16)
    rest = x - high.astype(F32)
    middle = rest.astype(jnp.bfloat16)
    return high, middle, (rest - middle.astype(F32)).astype(jnp.bfloat16)


def plain(a, b, ca=1, cb=0):
    return lax.dot_general(a, b, (((ca,), (cb,)), ((), ())), preferred_element_type=F32)


def left(parts, dim):
    high, middle, low = parts
    return jnp.concatenate([high, high, middle, high, low, middle], axis=dim)


def right(parts):
    high, middle, low = parts
    return jnp.concatenate([high, middle, high, low, high, middle], axis=0)


def stacked(a, b):
    return plain(left(thirds(a), 0), right(thirds(b)), 0, 0)


def two_thirds(a, b):
    ah, am, _ = thirds(a)
    bh, bm, _ = thirds(b)
    rows = a.shape[0]
    both = plain(jnp.concatenate([ah, am], axis=0), bh)
    return both[:rows] + (both[rows:] + plain(ah, bm))


def lane_copy(tile, lane):
    return jnp.broadcast_to(tile[:, lane : lane + 1], tile.shape)


def row_copy(tile, row):
    return jnp.broadcast_to(tile[row : row + 1, :], tile.shape)


def iotas(shape):
    return lax.broadcasted_iota(jnp.int32, shape, 0), lax.broadcasted_iota(jnp.int32, shape, 1)


def eliminate(tiles, base):
    tiles = list(tiles)
    steps = len(tiles)
    sub, lane = iotas((TILE, BLOCK))
    cols = [lane_copy(tiles[0], base + j) for j in range(TILE)]
    out = []
    for s in range(steps):
        k = base + TILE * s
        tile = tiles[s]
        inside = (lane >= k) & (lane < k + TILE)
        scale, low = [], {}
        for j in range(TILE):
            scale.append(lax.rsqrt(row_copy(cols[j], j)))
            column = cols[j] * scale[j]
            for i in range(j + 1, TILE):
                low[i, j] = row_copy(column, i)
            for c in range(j + 1, TILE):
                cols[c] = cols[c] - column * low[c, j]
        rows = []
        for i in range(TILE):
            row = jnp.where(inside, jnp.where(lane == k + i, 1.0, 0.0), row_copy(tile, i))
            for m in range(i):
                row = row - low[i, m] * rows[m]
            rows.append(row * scale[i])
        new = rows[0]
        for i in range(1, TILE):
            new = jnp.where(sub == i, rows[i], new)
        out.append(new)
        for g in range(s + 1, steps):
            t = tiles[g]
            w = []
            for j in range(TILE):
                acc = lane_copy(t, k + j)
                for m in range(j):
                    acc = acc - low[j, m] * w[m]
                w.append(acc * scale[j])
            if g == s + 1:
                cols = [lane_copy(t, k + TILE + c) for c in range(TILE)]
                for c in range(TILE):
                    for i in range(TILE):
                        cols[c] = cols[c] - w[i] * row_copy(w[i], c)
            t = jnp.where(inside, 0.0, t)
            for i in range(TILE):
                t = t - w[i] * rows[i]
            tiles[g] = t
    return out


def inverse_factor(tiles, size):
    tiles = list(tiles)
    out = []
    count = size // TILE
    _, lane = iotas((TILE, BLOCK))
    for base in range(0, len(tiles) * TILE, size):
        done = eliminate(tiles[:count], base)
        out += done
        tiles = tiles[count:]
        if tiles:
            rows = jnp.concatenate(done, axis=0)
            place, at = iotas(rows.shape)
            keep = (at <= place + base) | (at >= base + size)
            update = stacked(rows, jnp.where(keep, rows, 0.0))
            for g in range(len(tiles)):
                start = base + size + TILE * g
                kept = jnp.where(lane < base + size, jnp.where(lane < base, tiles[g], 0.0), tiles[g])
                tiles[g] = kept - update[start : start + TILE, :]
    sub, _ = iotas((TILE, BLOCK))
    return [jnp.where(lane <= TILE * s + sub, t, 0.0) for s, t in enumerate(out)]


def layout(nb):
    shared = [(i, i) for i in range(0, nb, 2)]
    return shared + [(i, j) for i in range(nb) for j in range(i + 1, nb)]


def pack(gram, count):
    nb = gram.shape[0] // BLOCK

    def block(i, j):
        return gram[i * BLOCK : (i + 1) * BLOCK, j * BLOCK : (j + 1) * BLOCK]

    row, lane = iotas((BLOCK, BLOCK))
    parts, extra = [], [jnp.full((1, BLOCK), count, F32)]
    for i, j in layout(nb):
        if i == j:
            second = block(i + 1, i + 1)
            parts.append(jnp.where(row <= lane, block(i, i), second))
            extra.append(jnp.sum(jnp.where(row == lane, second, 0.0), axis=0, keepdims=True))
        else:
            parts.append(block(i, j))
    fill = jnp.zeros((-len(extra) % TILE, BLOCK), F32)
    extra = jnp.concatenate(extra + [fill], axis=0)
    parts = jnp.concatenate(parts, axis=0)
    parts = parts.reshape(4, parts.shape[0] // 4, BLOCK)
    return jnp.concatenate([parts, jnp.broadcast_to(extra, (4,) + extra.shape)], axis=1)


def unpack(read, nb, put):
    quarter = nb * nb * BLOCK // 8
    row, lane = iotas((BLOCK, BLOCK))
    inverse = 1.0 / read(0, quarter, 1)

    def block(t):
        halves = []
        for start in (t * BLOCK, t * BLOCK + BLOCK // 2):
            part, offset = divmod(start, quarter)
            halves.append(read(part, offset, BLOCK // 2) * inverse)
        return jnp.concatenate(halves, axis=0)

    for t, (i, j) in enumerate(layout(nb)):
        if i == j:
            both = block(t)
            turned = both.T
            ends = read(0, quarter + 1 + i // 2, 1) * inverse
            put(i, i, jnp.where(row <= lane, both, turned))
            second = jnp.where(row > lane, both, turned)
            put(i + 1, i + 1, jnp.where(row == lane, ends, second))
        else:
            put(i, j, block(t))


def span(i):
    return slice(i * BLOCK, (i + 1) * BLOCK)


def factor_kernel(mine_ref, x_hbm, y_ref, s_ref, x_ref, sem):
    @pl.when(lax.axis_index("field") == 0)
    def _():
        y_ref[...] = jnp.zeros_like(y_ref)

    @pl.when(lax.axis_index("field") == 1)
    def _():
        apply_factor(mine_ref, x_hbm, y_ref, s_ref, x_ref, sem)


def apply_factor(mine_ref, x_hbm, y_ref, s_ref, x_ref, sem):
    copy = pltpu.make_async_copy(x_hbm, x_ref, sem)
    copy.start()
    n = x_ref.shape[1]
    nb = n // BLOCK

    def read(part, start, rows):
        return mine_ref[part, start : start + rows, :]

    def put(i, j, v):
        s_ref[span(i), span(j)] = v

    unpack(read, nb, put)
    for b in range(nb):
        lo, hi = b * BLOCK, (b + 1) * BLOCK
        tiles = [s_ref[lo + r : lo + r + TILE, lo:hi] for r in range(0, BLOCK, TILE)]
        inverse = left(thirds(jnp.concatenate(inverse_factor(tiles, HALF), axis=0)), 1)

        def upper(columns):
            return thirds(plain(inverse, right(thirds(s_ref[lo:hi, columns]))))

        panels = []
        for start, stop in ((hi, hi + BLOCK), (hi + BLOCK, n)):
            if start < n:
                panels.append((start, upper(slice(start, stop))))
                if start == hi:
                    near = left(panels[0][1], 0)
                s_ref[span(b + 1), start:stop] -= plain(near, right(panels[-1][1]), 0, 0)
        if hi + BLOCK < n:
            far = panels[1][1]
            for r in range(0, n - hi - BLOCK, BLOCK):
                rows = slice(hi + BLOCK + r, hi + 2 * BLOCK + r)
                s_ref[rows, rows.start :] -= plain(
                    left([p[:, r : r + BLOCK] for p in far], 0),
                    right([p[:, r:] for p in far]), 0, 0,
                )
        panels.append((lo, upper(slice(lo, hi))))
        if b == 0:
            copy.wait()
        xh, xm, _ = thirds(x_ref[:, lo:hi])
        x = jnp.concatenate([xh, xm, xh], axis=1)
        for start, (uh, um, _) in panels:
            product = plain(x, jnp.concatenate([uh, uh, um], axis=0))
            columns = slice(start, start + uh.shape[1])
            y_ref[:, columns] = product if b == 0 else y_ref[:, columns] + product


def finish_kernel(
    valid_ref, mine_ref, other_ref, y_ref, y_other_ref, values_hbm, out_ref, strengths_ref,
    g_ref, values_ref, sem,
):
    copy = pltpu.make_async_copy(values_hbm, values_ref, sem)
    copy.start()
    modes, n = y_ref.shape
    nb = n // BLOCK
    first = lax.axis_index("field") == 0
    for f in range(2):

        def read(part, start, rows, f=f):
            a = mine_ref[part, start : start + rows, :]
            b = other_ref[part, start : start + rows, :]
            return jnp.where(first, a, b) if f == 0 else jnp.where(first, b, a)

        def put(i, j, v, f=f):
            g_ref[f, span(i), span(j)] = v
            if i != j:
                g_ref[f, span(j), span(i)] = v.T

        unpack(read, nb, put)

    def normal(product):
        wide = jnp.concatenate([product, jnp.zeros((modes, BLOCK - modes), F32)], axis=1)
        tiles = [wide[r : r + TILE, :] for r in range(0, modes, TILE)]
        return jnp.concatenate(inverse_factor(tiles, modes), axis=0)[:, :modes]

    y = jnp.where(first, y_other_ref[...], y_ref[...])
    t = two_thirds(y, g_ref[0])
    inverse = normal(dot(y, t, 1, 1))
    q0 = two_thirds(inverse, y)
    z = two_thirds(inverse, t)
    w = two_thirds(z, g_ref[1])
    inverse = normal(dot(z, w, 1, 1))
    q1 = two_thirds(inverse, z)
    row, lane = iotas((modes, modes))
    diagonal = jnp.sum(jnp.where(row == lane, inverse, 0.0), axis=0, keepdims=True)
    strengths_ref[...] = 1.0 / diagonal
    q = jnp.where(first, q0, q1)
    high = q.astype(jnp.bfloat16)
    low = (q - high.astype(F32)).astype(jnp.bfloat16)
    both = jnp.concatenate([high, low], axis=0)
    copy.wait()
    ocean = valid_ref[0, 0]
    points = values_ref.shape[0]
    step = min(points, 256)
    for r in range(0, points, step):
        product = lax.dot_general(
            both, values_ref[r : r + step, :], (((1,), (1,)), ((), ())),
            preferred_element_type=F32,
        )
        total = product[:modes] + product[modes:]
        _, place = iotas(total.shape)
        out_ref[:, r : r + step] = jnp.where(place + r < ocean, total, 0.0)


AXES = ("field", "group", "row")


def swap(value, which):
    sizes = [lax.axis_size(a) for a in AXES]
    moves = []
    for f in range(sizes[0]):
        for g in range(sizes[1]):
            for r in range(sizes[2]):
                there = dict(zip(AXES, (f, g, r)))
                for axis, b in which(f):
                    there[axis] ^= 1 << b
                here = (f * sizes[1] + g) * sizes[2] + r
                moves.append(
                    (here, (there["field"] * sizes[1] + there["group"]) * sizes[2] + there["row"])
                )
    return lax.ppermute(value, AXES, moves)


def has_bit(which):
    def of(f):
        axis, b = which(f)
        return (lax.axis_index(axis) >> b) & 1

    return jnp.where(lax.axis_index("field") == 0, of(0), of(1))


def sum_all(value):
    sizes = {axis: lax.axis_size(axis) for axis in ("row", "group")}
    if any(n & (n - 1) for n in sizes.values()) or min(sizes.values()) < 2:
        return lax.psum(value, ("group", "row"))
    bits = {axis: n.bit_length() - 1 for axis, n in sizes.items()}
    order = [("row", 0), ("group", 0)]
    order += [(axis, b) for axis in ("row", "group") for b in range(1, bits[axis])]
    steps = [lambda f, k=k: order[(k + 2 * (1 - f)) % len(order)] for k in range(len(order))]
    me = has_bit(steps[0]) + 2 * has_bit(steps[1])

    def turned(d):
        return lambda f: [steps[k](f) for k in range(2) if d >> k & 1]

    others = (3, 1, 2)
    arrived = [
        swap(lax.dynamic_slice_in_dim(value, me ^ d, 1, 0), turned(d)) for d in others
    ]
    part = lax.dynamic_slice_in_dim(value, me, 1, 0)
    for piece in arrived:
        part = part + piece
    for step in steps[2:]:
        part = part + swap(part, lambda f, step=step: [step(f)])
    held = {0: part} | {d: swap(part, turned(d)) for d in others}
    parts = []
    for q in range(4):
        chosen = held[q]
        for p in range(1, 4):
            chosen = jnp.where(me == p, held[q ^ p], chosen)
        parts.append(chosen)
    return jnp.concatenate(parts, axis=0)


def per_device(anomalies, valid_rows, start_basis):
    values = anomalies[0]
    rows_here, n = values.shape
    modes = start_basis.shape[1]
    ocean = valid_rows[0, 0]
    place = lax.broadcasted_iota(jnp.int32, (rows_here, 1), 0)
    masked = jnp.where(place < ocean, values, jnp.zeros_like(values))
    gram = lax.dot_general(
        masked, masked, (((0,), (0,)), ((), ())), preferred_element_type=F32
    )
    mine = sum_all(pack(gram, ocean.astype(F32)))
    y = pl.pallas_call(
        factor_kernel,
        out_shape=jax.ShapeDtypeStruct((modes, n), F32),
        in_specs=[VMEM, pl.BlockSpec(memory_space=pltpu.HBM)],
        out_specs=VMEM,
        scratch_shapes=[
            pltpu.VMEM((n, n), F32),
            pltpu.VMEM((modes, n), F32),
            pltpu.SemaphoreType.DMA,
        ],
        compiler_params=pltpu.CompilerParams(vmem_limit_bytes=GRANT),
    )(mine, start_basis.T)
    y, mine = lax.optimization_barrier((y, mine))
    partner = lambda f: [("field", 0)]
    y_other = swap(y, partner)
    other = swap(mine, partner)
    patterns, strengths = pl.pallas_call(
        finish_kernel,
        out_shape=(
            jax.ShapeDtypeStruct((modes, rows_here), F32),
            jax.ShapeDtypeStruct((1, modes), F32),
        ),
        in_specs=[SMEM, VMEM, VMEM, VMEM, VMEM, pl.BlockSpec(memory_space=pl.ANY)],
        out_specs=(VMEM, VMEM),
        scratch_shapes=[
            pltpu.VMEM((2, n, n), F32),
            pltpu.VMEM((rows_here, n), jnp.bfloat16),
            pltpu.SemaphoreType.DMA,
        ],
        compiler_params=pltpu.CompilerParams(vmem_limit_bytes=GRANT),
    )(valid_rows, mine, other, y, y_other, values)
    return patterns.T[None], strengths[0]


def solution(mesh):
    in_specs = (P("field", ("group", "row"), None), P("field", ("group", "row")), P())
    out_specs = (P("field", ("group", "row"), None), P())
    return jax.shard_map(
        per_device, mesh=mesh, in_specs=in_specs, out_specs=out_specs, check_vma=False
    )
```

```python
import jax
import jax.numpy as jnp
from jax import lax
from jax.experimental import pallas as pl
from jax.experimental.pallas import tpu as pltpu
from jax.sharding import PartitionSpec as P

HIGH = lax.Precision.HIGHEST
F32 = jnp.float32
BLOCK = 128
TILE = 8
HALF = 64
GRANT = 16 * 2**20
VMEM = pl.BlockSpec(memory_space=pltpu.VMEM)
SMEM = pl.BlockSpec(memory_space=pltpu.SMEM)


def dot(a, b, ca=1, cb=0):
    return lax.dot_general(
        a, b, (((ca,), (cb,)), ((), ())), precision=HIGH, preferred_element_type=F32
    )


def thirds(x):
    high = x.astype(jnp.bfloat16)
    rest = x - high.astype(F32)
    middle = rest.astype(jnp.bfloat16)
    return high, middle, (rest - middle.astype(F32)).astype(jnp.bfloat16)


def plain(a, b, ca=1, cb=0):
    return lax.dot_general(a, b, (((ca,), (cb,)), ((), ())), preferred_element_type=F32)


def left(parts, dim):
    high, middle, low = parts
    return jnp.concatenate([high, high, middle, high, low, middle], axis=dim)


def right(parts):
    high, middle, low = parts
    return jnp.concatenate([high, middle, high, low, high, middle], axis=0)


def stacked(a, b):
    return plain(left(thirds(a), 0), right(thirds(b)), 0, 0)


def two_thirds(a, b):
    ah, am, _ = thirds(a)
    bh, bm, _ = thirds(b)
    rows = a.shape[0]
    both = plain(jnp.concatenate([ah, am], axis=0), bh)
    return both[:rows] + (both[rows:] + plain(ah, bm))


def lane_copy(tile, lane):
    return jnp.broadcast_to(tile[:, lane : lane + 1], tile.shape)


def row_copy(tile, row):
    return jnp.broadcast_to(tile[row : row + 1, :], tile.shape)


def iotas(shape):
    return lax.broadcasted_iota(jnp.int32, shape, 0), lax.broadcasted_iota(jnp.int32, shape, 1)


def eliminate(tiles, base):
    tiles = list(tiles)
    steps = len(tiles)
    sub, lane = iotas((TILE, BLOCK))
    cols = [lane_copy(tiles[0], base + j) for j in range(TILE)]
    out = []
    for s in range(steps):
        k = base + TILE * s
        tile = tiles[s]
        inside = (lane >= k) & (lane < k + TILE)
        scale, low = [], {}
        for j in range(TILE):
            scale.append(lax.rsqrt(row_copy(cols[j], j)))
            column = cols[j] * scale[j]
            for i in range(j + 1, TILE):
                low[i, j] = row_copy(column, i)
            for c in range(j + 1, TILE):
                cols[c] = cols[c] - column * low[c, j]
        rows = []
        for i in range(TILE):
            row = jnp.where(inside, jnp.where(lane == k + i, 1.0, 0.0), row_copy(tile, i))
            for m in range(i):
                row = row - low[i, m] * rows[m]
            rows.append(row * scale[i])
        new = rows[0]
        for i in range(1, TILE):
            new = jnp.where(sub == i, rows[i], new)
        out.append(new)
        for g in range(s + 1, steps):
            t = tiles[g]
            w = []
            for j in range(TILE):
                acc = lane_copy(t, k + j)
                for m in range(j):
                    acc = acc - low[j, m] * w[m]
                w.append(acc * scale[j])
            if g == s + 1:
                cols = [lane_copy(t, k + TILE + c) for c in range(TILE)]
                for c in range(TILE):
                    for i in range(TILE):
                        cols[c] = cols[c] - w[i] * row_copy(w[i], c)
            t = jnp.where(inside, 0.0, t)
            for i in range(TILE):
                t = t - w[i] * rows[i]
            tiles[g] = t
    return out


def inverse_factor(tiles, size, between=lambda: None):
    tiles = list(tiles)
    out = []
    count = size // TILE
    _, lane = iotas((TILE, BLOCK))
    for base in range(0, len(tiles) * TILE, size):
        done = eliminate(tiles[:count], base)
        out += done
        if base == 0:
            between()
        tiles = tiles[count:]
        if tiles:
            rows = jnp.concatenate(done, axis=0)
            place, at = iotas(rows.shape)
            keep = (at <= place + base) | (at >= base + size)
            update = stacked(rows, jnp.where(keep, rows, 0.0))
            for g in range(len(tiles)):
                start = base + size + TILE * g
                kept = jnp.where(lane < base + size, jnp.where(lane < base, tiles[g], 0.0), tiles[g])
                tiles[g] = kept - update[start : start + TILE, :]
    sub, _ = iotas((TILE, BLOCK))
    return [jnp.where(lane <= TILE * s + sub, t, 0.0) for s, t in enumerate(out)]


def layout(nb):
    shared = [(i, i) for i in range(0, nb, 2)]
    return shared + [(i, j) for i in range(nb) for j in range(i + 1, nb)]


def pack(gram, count):
    nb = gram.shape[0] // BLOCK

    def block(i, j):
        return gram[i * BLOCK : (i + 1) * BLOCK, j * BLOCK : (j + 1) * BLOCK]

    row, lane = iotas((BLOCK, BLOCK))
    parts, extra = [], [jnp.full((1, BLOCK), count, F32)]
    for i, j in layout(nb):
        if i == j:
            second = block(i + 1, i + 1)
            parts.append(jnp.where(row <= lane, block(i, i), second))
            extra.append(jnp.sum(jnp.where(row == lane, second, 0.0), axis=0, keepdims=True))
        else:
            parts.append(block(i, j))
    fill = jnp.zeros((-len(extra) % TILE, BLOCK), F32)
    extra = jnp.concatenate(extra + [fill], axis=0)
    parts = jnp.concatenate(parts, axis=0)
    parts = parts.reshape(4, parts.shape[0] // 4, BLOCK)
    return jnp.concatenate([parts, jnp.broadcast_to(extra, (4,) + extra.shape)], axis=1)


def unpack(read, nb, put):
    quarter = nb * nb * BLOCK // 8
    row, lane = iotas((BLOCK, BLOCK))
    inverse = 1.0 / read(0, quarter, 1)

    def block(t):
        halves = []
        for start in (t * BLOCK, t * BLOCK + BLOCK // 2):
            part, offset = divmod(start, quarter)
            halves.append(read(part, offset, BLOCK // 2) * inverse)
        return jnp.concatenate(halves, axis=0)

    for t, (i, j) in enumerate(layout(nb)):
        if i == j:
            both = block(t)
            turned = both.T
            ends = read(0, quarter + 1 + i // 2, 1) * inverse
            put(i, i, jnp.where(row <= lane, both, turned))
            second = jnp.where(row > lane, both, turned)
            put(i + 1, i + 1, jnp.where(row == lane, ends, second))
        else:
            put(i, j, block(t))


def span(i):
    return slice(i * BLOCK, (i + 1) * BLOCK)


def factor_kernel(mine_ref, x_hbm, y_ref, s_ref, x_ref, sem):
    @pl.when(lax.axis_index("field") == 0)
    def _():
        y_ref[...] = jnp.zeros_like(y_ref)

    @pl.when(lax.axis_index("field") == 1)
    def _():
        apply_factor(mine_ref, x_hbm, y_ref, s_ref, x_ref, sem)


def apply_factor(mine_ref, x_hbm, y_ref, s_ref, x_ref, sem):
    copy = pltpu.make_async_copy(x_hbm, x_ref, sem)
    copy.start()
    n = x_ref.shape[1]
    nb = n // BLOCK

    def read(part, start, rows):
        return mine_ref[part, start : start + rows, :]

    def put(i, j, v):
        s_ref[span(i), span(j)] = v

    unpack(read, nb, put)
    later = lambda: None
    for b in range(nb):
        lo, hi = b * BLOCK, (b + 1) * BLOCK
        far = hi + BLOCK
        tiles = [s_ref[lo + r : lo + r + TILE, lo:hi] for r in range(0, BLOCK, TILE)]
        inverse = jnp.concatenate(inverse_factor(tiles, HALF, later), axis=0)
        inverse = left(thirds(inverse), 1)

        def upper(start, stop, inverse=inverse, lo=lo, hi=hi):
            return thirds(plain(inverse, right(thirds(s_ref[lo:hi, start:stop]))))

        near = None
        if hi < n:
            near = upper(hi, far)
            s_ref[span(b + 1), hi:far] -= plain(left(near, 0), right(near), 0, 0)

        def later(b=b, lo=lo, hi=hi, far=far, near=near, upper=upper):
            panels = [] if near is None else [(hi, near)]
            if far < n:
                rest = upper(far, n)
                panels.append((far, rest))
                s_ref[hi:far, far:] -= plain(left(near, 0), right(rest), 0, 0)
                for r in range(0, n - far, BLOCK):
                    s_ref[far + r : far + r + BLOCK, far + r :] -= plain(
                        left([p[:, r : r + BLOCK] for p in rest], 0),
                        right([p[:, r:] for p in rest]), 0, 0,
                    )
            panels.append((lo, upper(lo, hi)))
            if b == 0:
                copy.wait()
            xh, xm, _ = thirds(x_ref[:, lo:hi])
            x = jnp.concatenate([xh, xm, xh], axis=1)
            for start, (uh, um, _) in panels:
                product = plain(x, jnp.concatenate([uh, uh, um], axis=0))
                columns = slice(start, start + uh.shape[1])
                y_ref[:, columns] = product if b == 0 else y_ref[:, columns] + product

    later()


def finish_kernel(
    valid_ref, mine_ref, other_ref, y_ref, y_other_ref, values_hbm, out_ref, strengths_ref,
    g_ref, values_ref, sem,
):
    copy = pltpu.make_async_copy(values_hbm, values_ref, sem)
    copy.start()
    modes, n = y_ref.shape
    nb = n // BLOCK
    first = lax.axis_index("field") == 0

    def fill(f):

        def read(part, start, rows):
            a = mine_ref[part, start : start + rows, :]
            b = other_ref[part, start : start + rows, :]
            return jnp.where(first, a, b) if f == 0 else jnp.where(first, b, a)

        def put(i, j, v):
            g_ref[f, span(i), span(j)] = v
            if i != j:
                g_ref[f, span(j), span(i)] = v.T

        unpack(read, nb, put)

    def normal(product):
        wide = jnp.concatenate([product, jnp.zeros((modes, BLOCK - modes), F32)], axis=1)
        tiles = [wide[r : r + TILE, :] for r in range(0, modes, TILE)]
        return jnp.concatenate(inverse_factor(tiles, modes), axis=0)[:, :modes]

    y = jnp.where(first, y_other_ref[...], y_ref[...])
    fill(0)
    t = two_thirds(y, g_ref[0])
    product = dot(y, t, 1, 1)
    fill(1)
    inverse = normal(product)
    q0 = two_thirds(inverse, y)
    z = two_thirds(inverse, t)
    w = two_thirds(z, g_ref[1])
    inverse = normal(dot(z, w, 1, 1))
    q1 = two_thirds(inverse, z)
    row, lane = iotas((modes, modes))
    diagonal = jnp.sum(jnp.where(row == lane, inverse, 0.0), axis=0, keepdims=True)
    strengths_ref[...] = 1.0 / diagonal
    q = jnp.where(first, q0, q1)
    high = q.astype(jnp.bfloat16)
    low = (q - high.astype(F32)).astype(jnp.bfloat16)
    both = jnp.concatenate([high, low], axis=0)
    copy.wait()
    ocean = valid_ref[0, 0]
    points = values_ref.shape[0]
    step = min(points, 256)
    for r in range(0, points, step):
        product = lax.dot_general(
            both, values_ref[r : r + step, :], (((1,), (1,)), ((), ())),
            preferred_element_type=F32,
        )
        total = product[:modes] + product[modes:]
        _, place = iotas(total.shape)
        out_ref[:, r : r + step] = jnp.where(place + r < ocean, total, 0.0)


AXES = ("field", "group", "row")


def swap(value, which):
    sizes = [lax.axis_size(a) for a in AXES]
    moves = []
    for f in range(sizes[0]):
        for g in range(sizes[1]):
            for r in range(sizes[2]):
                there = dict(zip(AXES, (f, g, r)))
                for axis, b in which(f):
                    there[axis] ^= 1 << b
                here = (f * sizes[1] + g) * sizes[2] + r
                moves.append(
                    (here, (there["field"] * sizes[1] + there["group"]) * sizes[2] + there["row"])
                )
    return lax.ppermute(value, AXES, moves)


def has_bit(which):
    def of(f):
        axis, b = which(f)
        return (lax.axis_index(axis) >> b) & 1

    return jnp.where(lax.axis_index("field") == 0, of(0), of(1))


def sum_all(value):
    sizes = {axis: lax.axis_size(axis) for axis in ("row", "group")}
    if any(n & (n - 1) for n in sizes.values()) or min(sizes.values()) < 2:
        return lax.psum(value, ("group", "row"))
    bits = {axis: n.bit_length() - 1 for axis, n in sizes.items()}
    order = [("row", 0), ("group", 0)]
    order += [(axis, b) for axis in ("row", "group") for b in range(1, bits[axis])]
    steps = [lambda f, k=k: order[(k + 2 * (1 - f)) % len(order)] for k in range(len(order))]
    me = has_bit(steps[0]) + 2 * has_bit(steps[1])

    def turned(d, first=0):
        return lambda f: [step(f) for k, step in enumerate(steps[first : first + 2]) if d >> k & 1]

    others = (3, 1, 2)
    arrived = [
        swap(lax.dynamic_slice_in_dim(value, me ^ d, 1, 0), turned(d)) for d in others
    ]
    part = lax.dynamic_slice_in_dim(value, me, 1, 0)
    for piece in arrived:
        part = part + piece
    for first in range(2, len(steps), 2):
        ways = (1, 2, 3) if first + 1 < len(steps) else (1,)
        arrived = [swap(part, turned(d, first)) for d in ways]
        for piece in arrived:
            part = part + piece
    held = {0: part} | {d: swap(part, turned(d)) for d in others}
    parts = []
    for q in range(4):
        chosen = held[q]
        for p in range(1, 4):
            chosen = jnp.where(me == p, held[q ^ p], chosen)
        parts.append(chosen)
    return jnp.concatenate(parts, axis=0)


def per_device(anomalies, valid_rows, start_basis):
    values = anomalies[0]
    rows_here, n = values.shape
    modes = start_basis.shape[1]
    ocean = valid_rows[0, 0]
    place = lax.broadcasted_iota(jnp.int32, (rows_here, 1), 0)
    masked = jnp.where(place < ocean, values, jnp.zeros_like(values))
    gram = lax.dot_general(
        masked, masked, (((0,), (0,)), ((), ())), preferred_element_type=F32
    )
    mine = sum_all(pack(gram, ocean.astype(F32)))
    y = pl.pallas_call(
        factor_kernel,
        out_shape=jax.ShapeDtypeStruct((modes, n), F32),
        in_specs=[VMEM, pl.BlockSpec(memory_space=pltpu.HBM)],
        out_specs=VMEM,
        scratch_shapes=[
            pltpu.VMEM((n, n), F32),
            pltpu.VMEM((modes, n), F32),
            pltpu.SemaphoreType.DMA,
        ],
        compiler_params=pltpu.CompilerParams(vmem_limit_bytes=GRANT),
    )(mine, pltpu.with_memory_space_constraint(start_basis.T, pltpu.HBM))
    y, mine = lax.optimization_barrier((y, mine))
    partner = lambda f: [("field", 0)]
    y_other = swap(y, partner)
    other = swap(mine, partner)
    patterns, strengths = pl.pallas_call(
        finish_kernel,
        out_shape=(
            jax.ShapeDtypeStruct((modes, rows_here), F32),
            jax.ShapeDtypeStruct((1, modes), F32),
        ),
        in_specs=[SMEM, VMEM, VMEM, VMEM, VMEM, pl.BlockSpec(memory_space=pl.ANY)],
        out_specs=(VMEM, VMEM),
        scratch_shapes=[
            pltpu.VMEM((2, n, n), F32),
            pltpu.VMEM((rows_here, n), jnp.bfloat16),
            pltpu.SemaphoreType.DMA,
        ],
        compiler_params=pltpu.CompilerParams(vmem_limit_bytes=GRANT),
    )(valid_rows, mine, other, y, y_other, values)
    return patterns.T[None], strengths[0]


def solution(mesh):
    in_specs = (P("field", ("group", "row"), None), P("field", ("group", "row")), P())
    out_specs = (P("field", ("group", "row"), None), P())
    return jax.shard_map(
        per_device, mesh=mesh, in_specs=in_specs, out_specs=out_specs, check_vma=False
    )
```

```python
import jax
import jax.numpy as jnp
from jax import lax
from jax.experimental import pallas as pl
from jax.experimental.pallas import tpu as pltpu
from jax.sharding import PartitionSpec as P

F32 = jnp.float32
BLOCK = 128
TILE = 8
HALF = 64
WIDE = 256
GRANT = 16 * 2**20
VMEM = pl.BlockSpec(memory_space=pltpu.VMEM)
SMEM = pl.BlockSpec(memory_space=pltpu.SMEM)


def thirds(x):
    high = x.astype(jnp.bfloat16)
    rest = x - high.astype(F32)
    middle = rest.astype(jnp.bfloat16)
    return high, middle, (rest - middle.astype(F32)).astype(jnp.bfloat16)


def plain(a, b, ca=1, cb=0):
    return lax.dot_general(a, b, (((ca,), (cb,)), ((), ())), preferred_element_type=F32)


def left(parts, dim):
    high, middle, low = parts
    return jnp.concatenate([high, high, middle, high, low, middle], axis=dim)


def right(parts):
    high, middle, low = parts
    return jnp.concatenate([high, middle, high, low, high, middle], axis=0)


def stacked(a, b):
    return plain(left(thirds(a), 0), right(thirds(b)), 0, 0)


def two_thirds(a, b):
    ah, am, _ = thirds(a)
    bh, bm, _ = thirds(b)
    rows = a.shape[0]
    both = plain(jnp.concatenate([ah, am], axis=0), bh)
    return both[:rows] + (both[rows:] + plain(ah, bm))


def rows_product(a, b):
    ah, am, al = thirds(a)
    bh, bm, bl = thirds(b)
    m = a.shape[0]
    p = plain(jnp.concatenate([ah, am, al], axis=0), bh, 1, 1)
    q = plain(jnp.concatenate([ah, am], axis=0), bm, 1, 1)
    return p[:m] + ((p[m : 2 * m] + q[:m]) + (p[2 * m :] + q[m:] + plain(ah, bl, 1, 1)))


def lane_copy(tile, lane):
    return jnp.broadcast_to(tile[:, lane : lane + 1], tile.shape)


def row_copy(tile, row):
    return jnp.broadcast_to(tile[row : row + 1, :], tile.shape)


def iotas(shape):
    return lax.broadcasted_iota(jnp.int32, shape, 0), lax.broadcasted_iota(jnp.int32, shape, 1)


def eliminate(tiles, base):
    tiles = list(tiles)
    steps = len(tiles)
    sub, lane = iotas((TILE, BLOCK))
    cols = [lane_copy(tiles[0], base + j) for j in range(TILE)]
    out = []
    for s in range(steps):
        k = base + TILE * s
        tile = tiles[s]
        inside = (lane >= k) & (lane < k + TILE)
        scale, low = [], {}
        for j in range(TILE):
            scale.append(lax.rsqrt(row_copy(cols[j], j)))
            column = cols[j] * scale[j]
            for i in range(j + 1, TILE):
                low[i, j] = row_copy(column, i)
            for c in range(j + 1, TILE):
                cols[c] = cols[c] - column * low[c, j]
        rows = []
        for i in range(TILE):
            row = jnp.where(inside, jnp.where(lane == k + i, 1.0, 0.0), row_copy(tile, i))
            for m in range(i):
                row = row - low[i, m] * rows[m]
            rows.append(row * scale[i])
        new = rows[0]
        for i in range(1, TILE):
            new = jnp.where(sub == i, rows[i], new)
        out.append(new)
        for g in range(s + 1, steps):
            t = tiles[g]
            w = []
            for j in range(TILE):
                acc = lane_copy(t, k + j)
                for m in range(j):
                    acc = acc - low[j, m] * w[m]
                w.append(acc * scale[j])
            if g == s + 1:
                cols = [lane_copy(t, k + TILE + c) for c in range(TILE)]
                for c in range(TILE):
                    for i in range(TILE):
                        cols[c] = cols[c] - w[i] * row_copy(w[i], c)
            t = jnp.where(inside, 0.0, t)
            for i in range(TILE):
                t = t - w[i] * rows[i]
            tiles[g] = t
    return out


def inverse_factor(tiles, size, between=lambda: None):
    tiles = list(tiles)
    out = []
    count = size // TILE
    _, lane = iotas((TILE, BLOCK))
    for base in range(0, len(tiles) * TILE, size):
        done = eliminate(tiles[:count], base)
        out += done
        if base == 0:
            between()
        tiles = tiles[count:]
        if tiles:
            rows = jnp.concatenate(done, axis=0)
            place, at = iotas(rows.shape)
            keep = (at <= place + base) | (at >= base + size)
            update = stacked(rows, jnp.where(keep, rows, 0.0))
            for g in range(len(tiles)):
                start = base + size + TILE * g
                kept = jnp.where(lane < base + size, jnp.where(lane < base, tiles[g], 0.0), tiles[g])
                tiles[g] = kept - update[start : start + TILE, :]
    sub, _ = iotas((TILE, BLOCK))
    return [jnp.where(lane <= TILE * s + sub, t, 0.0) for s, t in enumerate(out)]


def layout(nb):
    shared = [(i, i) for i in range(0, nb, 2)]
    return shared + [(i, j) for i in range(nb) for j in range(i + 1, nb)]


def gram_kernel(valid_ref, values_hbm, out_ref, values_ref, gram_ref, sem):
    copy = pltpu.make_async_copy(values_hbm, values_ref, sem)
    copy.start()
    points, n = values_ref.shape
    nb = n // BLOCK
    ocean = valid_ref[0, 0]
    place, _ = iotas((points, n))
    copy.wait()
    masked = jnp.where(place < ocean, values_ref[...].astype(F32), 0.0).astype(jnp.bfloat16)
    for start in range(0, n, WIDE):
        stop = min(start + WIDE, n)
        gram_ref[start:stop, start:] = plain(masked[:, start:stop], masked[:, start:], 0, 0)
    row, lane = iotas((BLOCK, BLOCK))
    quarter = nb * nb * BLOCK // 8
    extra = [jnp.full((1, BLOCK), ocean.astype(F32))]
    for t, (i, j) in enumerate(layout(nb)):
        block = gram_ref[span(i), span(j)]
        if i == j:
            second = gram_ref[span(i + 1), span(i + 1)]
            block = jnp.where(row <= lane, block, second)
            extra.append(jnp.sum(jnp.where(row == lane, second, 0.0), axis=0, keepdims=True))
        half = BLOCK // 2
        for h in range(2):
            part, offset = divmod(t * BLOCK + half * h, quarter)
            out_ref[part, offset : offset + half, :] = block[half * h : half * (h + 1)]
    fill = jnp.zeros((-len(extra) % TILE, BLOCK), F32)
    extra = jnp.concatenate(extra + [fill], axis=0)
    for part in range(4):
        out_ref[part, quarter:, :] = extra


def unpack(read, nb, put):
    quarter = nb * nb * BLOCK // 8
    row, lane = iotas((BLOCK, BLOCK))
    inverse = 1.0 / read(0, quarter, 1)

    def block(t):
        halves = []
        for start in (t * BLOCK, t * BLOCK + BLOCK // 2):
            part, offset = divmod(start, quarter)
            halves.append(read(part, offset, BLOCK // 2) * inverse)
        return jnp.concatenate(halves, axis=0)

    for t, (i, j) in enumerate(layout(nb)):
        if i == j:
            both = block(t)
            turned = both.T
            ends = read(0, quarter + 1 + i // 2, 1) * inverse
            put(i, i, jnp.where(row <= lane, both, turned))
            second = jnp.where(row > lane, both, turned)
            put(i + 1, i + 1, jnp.where(row == lane, ends, second))
        else:
            put(i, j, block(t))


def span(i):
    return slice(i * BLOCK, (i + 1) * BLOCK)


def factor_kernel(mine_ref, x_hbm, y_ref, s_ref, x_ref, sem):
    @pl.when(lax.axis_index("field") == 0)
    def _():
        y_ref[...] = jnp.zeros_like(y_ref)

    @pl.when(lax.axis_index("field") == 1)
    def _():
        apply_factor(mine_ref, x_hbm, y_ref, s_ref, x_ref, sem)


def apply_factor(mine_ref, x_hbm, y_ref, s_ref, x_ref, sem):
    copy = pltpu.make_async_copy(x_hbm, x_ref, sem)
    copy.start()
    n = x_ref.shape[1]
    nb = n // BLOCK

    def read(part, start, rows):
        return mine_ref[part, start : start + rows, :]

    def put(i, j, v):
        s_ref[span(i), span(j)] = v

    unpack(read, nb, put)
    later = lambda: None
    for b in range(nb):
        lo, hi = b * BLOCK, (b + 1) * BLOCK
        far = hi + BLOCK
        tiles = [s_ref[lo + r : lo + r + TILE, lo:hi] for r in range(0, BLOCK, TILE)]
        inverse = jnp.concatenate(inverse_factor(tiles, HALF, later), axis=0)
        inverse = left(thirds(inverse), 1)

        def upper(start, stop, inverse=inverse, lo=lo, hi=hi):
            return thirds(plain(inverse, right(thirds(s_ref[lo:hi, start:stop]))))

        near = None
        if hi < n:
            near = upper(hi, far)
            s_ref[span(b + 1), hi:far] -= plain(left(near, 0), right(near), 0, 0)

        def later(b=b, lo=lo, hi=hi, far=far, near=near, upper=upper):
            panels = [] if near is None else [(hi, near)]
            if far < n:
                rest = upper(far, n)
                panels.append((far, rest))
                s_ref[hi:far, far:] -= plain(left(near, 0), right(rest), 0, 0)
                for r in range(0, n - far, BLOCK):
                    s_ref[far + r : far + r + BLOCK, far + r :] -= plain(
                        left([p[:, r : r + BLOCK] for p in rest], 0),
                        right([p[:, r:] for p in rest]), 0, 0,
                    )
            panels.append((lo, upper(lo, hi)))
            if b == 0:
                copy.wait()
            xh, xm, _ = thirds(x_ref[:, lo:hi])
            x = jnp.concatenate([xh, xm, xh], axis=1)
            for start, (uh, um, _) in panels:
                product = plain(x, jnp.concatenate([uh, uh, um], axis=0))
                columns = slice(start, start + uh.shape[1])
                y_ref[:, columns] = product if b == 0 else y_ref[:, columns] + product

    later()


def finish_kernel(
    valid_ref, mine_ref, other_ref, y_ref, y_other_ref, values_hbm, out_ref, strengths_ref,
    g_ref, values_ref, sem,
):
    copy = pltpu.make_async_copy(values_hbm, values_ref, sem)
    copy.start()
    modes, n = y_ref.shape
    nb = n // BLOCK
    first = lax.axis_index("field") == 0

    def fill(f):

        def read(part, start, rows):
            a = mine_ref[part, start : start + rows, :]
            b = other_ref[part, start : start + rows, :]
            return jnp.where(first, a, b) if f == 0 else jnp.where(first, b, a)

        def put(i, j, v):
            g_ref[f, span(i), span(j)] = v
            if i != j:
                g_ref[f, span(j), span(i)] = v.T

        unpack(read, nb, put)

    def normal(product):
        wide = jnp.concatenate([product, jnp.zeros((modes, BLOCK - modes), F32)], axis=1)
        tiles = [wide[r : r + TILE, :] for r in range(0, modes, TILE)]
        return jnp.concatenate(inverse_factor(tiles, modes), axis=0)[:, :modes]

    y = jnp.where(first, y_other_ref[...], y_ref[...])
    fill(0)
    t = two_thirds(y, g_ref[0])
    product = rows_product(y, t)
    fill(1)
    inverse = normal(product)
    q0 = two_thirds(inverse, y)
    z = two_thirds(inverse, t)
    w = two_thirds(z, g_ref[1])
    inverse = normal(rows_product(z, w))
    q1 = two_thirds(inverse, z)
    row, lane = iotas((modes, modes))
    diagonal = jnp.sum(jnp.where(row == lane, inverse, 0.0), axis=0, keepdims=True)
    strengths_ref[...] = 1.0 / diagonal
    q = jnp.where(first, q0, q1)
    high = q.astype(jnp.bfloat16)
    low = (q - high.astype(F32)).astype(jnp.bfloat16)
    both = jnp.concatenate([high, low], axis=0)
    copy.wait()
    ocean = valid_ref[0, 0]
    points = values_ref.shape[0]
    step = min(points, 256)
    for r in range(0, points, step):
        product = lax.dot_general(
            both, values_ref[r : r + step, :], (((1,), (1,)), ((), ())),
            preferred_element_type=F32,
        )
        total = product[:modes] + product[modes:]
        _, place = iotas(total.shape)
        out_ref[:, r : r + step] = jnp.where(place + r < ocean, total, 0.0)


AXES = ("field", "group", "row")


def swap(value, which):
    sizes = [lax.axis_size(a) for a in AXES]
    moves = []
    for f in range(sizes[0]):
        for g in range(sizes[1]):
            for r in range(sizes[2]):
                there = dict(zip(AXES, (f, g, r)))
                for axis, b in which(f):
                    there[axis] ^= 1 << b
                here = (f * sizes[1] + g) * sizes[2] + r
                moves.append(
                    (here, (there["field"] * sizes[1] + there["group"]) * sizes[2] + there["row"])
                )
    return lax.ppermute(value, AXES, moves)


def has_bit(which):
    def of(f):
        axis, b = which(f)
        return (lax.axis_index(axis) >> b) & 1

    return jnp.where(lax.axis_index("field") == 0, of(0), of(1))


def sum_all(value):
    sizes = {axis: lax.axis_size(axis) for axis in ("row", "group")}
    if any(n & (n - 1) for n in sizes.values()) or min(sizes.values()) < 2:
        return lax.psum(value, ("group", "row"))
    bits = {axis: n.bit_length() - 1 for axis, n in sizes.items()}
    order = [("row", 0), ("group", 0)]
    order += [(axis, b) for axis in ("row", "group") for b in range(1, bits[axis])]
    steps = [lambda f, k=k: order[(k + 2 * (1 - f)) % len(order)] for k in range(len(order))]
    me = has_bit(steps[0]) + 2 * has_bit(steps[1])

    def turned(d, first=0):
        return lambda f: [step(f) for k, step in enumerate(steps[first : first + 2]) if d >> k & 1]

    others = (3, 1, 2)
    arrived = [
        swap(lax.dynamic_slice_in_dim(value, me ^ d, 1, 0), turned(d)) for d in others
    ]
    part = lax.dynamic_slice_in_dim(value, me, 1, 0)
    for piece in arrived:
        part = part + piece
    for first in range(2, len(steps), 2):
        ways = (1, 2, 3) if first + 1 < len(steps) else (1,)
        arrived = [swap(part, turned(d, first)) for d in ways]
        for piece in arrived:
            part = part + piece
    held = {0: part} | {d: swap(part, turned(d)) for d in others}
    parts = []
    for q in range(4):
        chosen = held[q]
        for p in range(1, 4):
            chosen = jnp.where(me == p, held[q ^ p], chosen)
        parts.append(chosen)
    return jnp.concatenate(parts, axis=0)


def per_device(anomalies, valid_rows, start_basis):
    values = anomalies[0]
    rows_here, n = values.shape
    modes = start_basis.shape[1]
    nb = n // BLOCK
    extra = -(-(1 + nb // 2) // TILE) * TILE
    packed = pl.pallas_call(
        gram_kernel,
        out_shape=jax.ShapeDtypeStruct((4, nb * nb * BLOCK // 8 + extra, BLOCK), F32),
        in_specs=[SMEM, pl.BlockSpec(memory_space=pltpu.HBM)],
        out_specs=VMEM,
        scratch_shapes=[
            pltpu.VMEM((rows_here, n), jnp.bfloat16),
            pltpu.VMEM((n, n), F32),
            pltpu.SemaphoreType.DMA,
        ],
        compiler_params=pltpu.CompilerParams(vmem_limit_bytes=GRANT),
    )(valid_rows, pltpu.with_memory_space_constraint(values, pltpu.HBM))
    mine = sum_all(packed)
    y = pl.pallas_call(
        factor_kernel,
        out_shape=jax.ShapeDtypeStruct((modes, n), F32),
        in_specs=[VMEM, pl.BlockSpec(memory_space=pltpu.HBM)],
        out_specs=VMEM,
        scratch_shapes=[
            pltpu.VMEM((n, n), F32),
            pltpu.VMEM((modes, n), F32),
            pltpu.SemaphoreType.DMA,
        ],
        compiler_params=pltpu.CompilerParams(vmem_limit_bytes=GRANT),
    )(mine, pltpu.with_memory_space_constraint(start_basis.T, pltpu.HBM))
    y, mine = lax.optimization_barrier((y, mine))
    partner = lambda f: [("field", 0)]
    y_other = swap(y, partner)
    other = swap(mine, partner)
    patterns, strengths = pl.pallas_call(
        finish_kernel,
        out_shape=(
            jax.ShapeDtypeStruct((modes, rows_here), F32),
            jax.ShapeDtypeStruct((1, modes), F32),
        ),
        in_specs=[SMEM, VMEM, VMEM, VMEM, VMEM, pl.BlockSpec(memory_space=pl.ANY)],
        out_specs=(VMEM, VMEM),
        scratch_shapes=[
            pltpu.VMEM((2, n, n), F32),
            pltpu.VMEM((rows_here, n), jnp.bfloat16),
            pltpu.SemaphoreType.DMA,
        ],
        compiler_params=pltpu.CompilerParams(vmem_limit_bytes=GRANT),
    )(valid_rows, mine, other, y, y_other, values)
    return patterns.T[None], strengths[0]


def solution(mesh):
    in_specs = (P("field", ("group", "row"), None), P("field", ("group", "row")), P())
    out_specs = (P("field", ("group", "row"), None), P())
    return jax.shard_map(
        per_device, mesh=mesh, in_specs=in_specs, out_specs=out_specs, check_vma=False
    )
```

```python
import jax
import jax.numpy as jnp
from jax import lax
from jax.experimental import pallas as pl
from jax.experimental.pallas import tpu as pltpu
from jax.sharding import PartitionSpec as P


F32 = jnp.float32
BLOCK = 128
TILE = 8
HALF = 64
WIDE = 256
GRANT = 16 * 2**20
VMEM = pl.BlockSpec(memory_space=pltpu.VMEM)
SMEM = pl.BlockSpec(memory_space=pltpu.SMEM)


def thirds(x):
    high = x.astype(jnp.bfloat16)
    rest = x - high.astype(F32)
    middle = rest.astype(jnp.bfloat16)
    return high, middle, (rest - middle.astype(F32)).astype(jnp.bfloat16)


def plain(a, b, ca=1, cb=0):
    return lax.dot_general(a, b, (((ca,), (cb,)), ((), ())), preferred_element_type=F32)


def left(parts, dim):
    high, middle, low = parts
    return jnp.concatenate([high, high, middle, high, low, middle], axis=dim)


def right(parts):
    high, middle, low = parts
    return jnp.concatenate([high, middle, high, low, high, middle], axis=0)


def stacked(a, b):
    return plain(left(thirds(a), 0), right(thirds(b)), 0, 0)


def two_thirds(a, b):
    ah, am, _ = thirds(a)
    bh, bm, _ = thirds(b)
    rows = a.shape[0]
    both = plain(jnp.concatenate([ah, am], axis=0), bh)
    return both[:rows] + (both[rows:] + plain(ah, bm))


def rows_product(a, b):
    ah, am, al = thirds(a)
    bh, bm, bl = thirds(b)
    m = a.shape[0]
    p = plain(jnp.concatenate([ah, am, al], axis=0), bh, 1, 1)
    q = plain(jnp.concatenate([ah, am], axis=0), bm, 1, 1)
    return p[:m] + ((p[m : 2 * m] + q[:m]) + (p[2 * m :] + q[m:] + plain(ah, bl, 1, 1)))


def lane_copy(tile, lane):
    return jnp.broadcast_to(tile[:, lane : lane + 1], tile.shape)


def row_copy(tile, row):
    return jnp.broadcast_to(tile[row : row + 1, :], tile.shape)


def iotas(shape):
    return lax.broadcasted_iota(jnp.int32, shape, 0), lax.broadcasted_iota(jnp.int32, shape, 1)


def eliminate(tiles, base):
    tiles = list(tiles)
    steps = len(tiles)
    sub, lane = iotas((TILE, BLOCK))
    cols = [lane_copy(tiles[0], base + j) for j in range(TILE)]
    out = []
    for s in range(steps):
        k = base + TILE * s
        tile = tiles[s]
        inside = (lane >= k) & (lane < k + TILE)
        scale, low = [], {}
        for j in range(TILE):
            scale.append(lax.rsqrt(row_copy(cols[j], j)))
            column = cols[j] * scale[j]
            for i in range(j + 1, TILE):
                low[i, j] = row_copy(column, i)
            for c in range(j + 1, TILE):
                cols[c] = cols[c] - column * low[c, j]
        rows = []
        for i in range(TILE):
            row = jnp.where(inside, jnp.where(lane == k + i, 1.0, 0.0), row_copy(tile, i))
            for m in range(i):
                row = row - low[i, m] * rows[m]
            rows.append(row * scale[i])
        new = rows[0]
        for i in range(1, TILE):
            new = jnp.where(sub == i, rows[i], new)
        out.append(new)
        for g in range(s + 1, steps):
            t = tiles[g]
            w = []
            for j in range(TILE):
                acc = lane_copy(t, k + j)
                for m in range(j):
                    acc = acc - low[j, m] * w[m]
                w.append(acc * scale[j])
            if g == s + 1:
                cols = [lane_copy(t, k + TILE + c) for c in range(TILE)]
                for c in range(TILE):
                    for i in range(TILE):
                        cols[c] = cols[c] - w[i] * row_copy(w[i], c)
            t = jnp.where(inside, 0.0, t)
            for i in range(TILE):
                t = t - w[i] * rows[i]
            tiles[g] = t
    return out


def inverse_factor(tiles, size, between=lambda: None):
    tiles = list(tiles)
    out = []
    count = size // TILE
    _, lane = iotas((TILE, BLOCK))
    for base in range(0, len(tiles) * TILE, size):
        done = eliminate(tiles[:count], base)
        out += done
        if base == 0:
            between()
        tiles = tiles[count:]
        if tiles:
            rows = jnp.concatenate(done, axis=0)
            place, at = iotas(rows.shape)
            keep = (at <= place + base) | (at >= base + size)
            update = stacked(rows, jnp.where(keep, rows, 0.0))
            for g in range(len(tiles)):
                start = base + size + TILE * g
                kept = jnp.where(lane < base + size, jnp.where(lane < base, tiles[g], 0.0), tiles[g])
                tiles[g] = kept - update[start : start + TILE, :]
    sub, _ = iotas((TILE, BLOCK))
    return [jnp.where(lane <= TILE * s + sub, t, 0.0) for s, t in enumerate(out)]


def layout(nb):
    shared = [(i, i) for i in range(0, nb, 2)]
    return shared + [(i, j) for i in range(nb) for j in range(i + 1, nb)]


def gram_kernel(valid_ref, values_hbm, out_ref, values_ref, gram_ref, sem):
    copy = pltpu.make_async_copy(values_hbm, values_ref, sem)
    copy.start()
    points, n = values_ref.shape
    nb = n // BLOCK
    ocean = valid_ref[0, 0]
    place, _ = iotas((points, n))
    copy.wait()
    masked = jnp.where(place < ocean, values_ref[...].astype(F32), 0.0).astype(jnp.bfloat16)
    for start in range(0, n, WIDE):
        stop = min(start + WIDE, n)
        gram_ref[start:stop, start:] = plain(masked[:, start:stop], masked[:, start:], 0, 0)
    row, lane = iotas((BLOCK, BLOCK))
    quarter = nb * nb * BLOCK // 8
    extra = [jnp.full((1, BLOCK), ocean.astype(F32))]
    for t, (i, j) in enumerate(layout(nb)):
        block = gram_ref[span(i), span(j)]
        if i == j:
            second = gram_ref[span(i + 1), span(i + 1)]
            block = jnp.where(row <= lane, block, second)
            extra.append(jnp.sum(jnp.where(row == lane, second, 0.0), axis=0, keepdims=True))
        half = BLOCK // 2
        for h in range(2):
            part, offset = divmod(t * BLOCK + half * h, quarter)
            out_ref[part, offset : offset + half, :] = block[half * h : half * (h + 1)]
    fill = jnp.zeros((-len(extra) % TILE, BLOCK), F32)
    extra = jnp.concatenate(extra + [fill], axis=0)
    for part in range(4):
        out_ref[part, quarter:, :] = extra


def unpack(read, nb, put):
    quarter = nb * nb * BLOCK // 8
    row, lane = iotas((BLOCK, BLOCK))
    inverse = 1.0 / read(0, quarter, 1)

    def block(t):
        halves = []
        for start in (t * BLOCK, t * BLOCK + BLOCK // 2):
            part, offset = divmod(start, quarter)
            halves.append(read(part, offset, BLOCK // 2) * inverse)
        return jnp.concatenate(halves, axis=0)

    for t, (i, j) in enumerate(layout(nb)):
        if i == j:
            both = block(t)
            turned = both.T
            ends = read(0, quarter + 1 + i // 2, 1) * inverse
            put(i, i, jnp.where(row <= lane, both, turned))
            second = jnp.where(row > lane, both, turned)
            put(i + 1, i + 1, jnp.where(row == lane, ends, second))
        else:
            put(i, j, block(t))


def span(i):
    return slice(i * BLOCK, (i + 1) * BLOCK)


def factor_kernel(mine_ref, x_hbm, out_ref, s_ref, y_ref, x_ref, sem, sems):
    parts, size, _ = mine_ref.shape
    copies = [
        pltpu.make_async_copy(mine_ref.at[p], out_ref.at[pl.ds(p * size, size)], sems.at[p])
        for p in range(parts)
    ]
    for copy in copies:
        copy.start()

    @pl.when(lax.axis_index("field") == 0)
    def _():
        y_ref[...] = jnp.zeros_like(y_ref)

    @pl.when(lax.axis_index("field") == 1)
    def _():
        apply_factor(mine_ref, x_hbm, y_ref, s_ref, x_ref, sem)

    modes, n = y_ref.shape
    for t in range(n // BLOCK):
        start = parts * size + t * modes
        out_ref[start : start + modes, :] = y_ref[:, span(t)]
    for copy in copies:
        copy.wait()


def apply_factor(mine_ref, x_hbm, y_ref, s_ref, x_ref, sem):
    copy = pltpu.make_async_copy(x_hbm, x_ref, sem)
    copy.start()
    n = x_ref.shape[1]
    nb = n // BLOCK

    def read(part, start, rows):
        return mine_ref[part, start : start + rows, :]

    def put(i, j, v):
        s_ref[span(i), span(j)] = v

    unpack(read, nb, put)
    later = lambda: None
    for b in range(nb):
        lo, hi = b * BLOCK, (b + 1) * BLOCK
        far = hi + BLOCK
        tiles = [s_ref[lo + r : lo + r + TILE, lo:hi] for r in range(0, BLOCK, TILE)]
        inverse = jnp.concatenate(inverse_factor(tiles, HALF, later), axis=0)
        inverse = left(thirds(inverse), 1)

        def upper(start, stop, inverse=inverse, lo=lo, hi=hi):
            return thirds(plain(inverse, right(thirds(s_ref[lo:hi, start:stop]))))

        near = None
        if hi < n:
            near = upper(hi, far)
            s_ref[span(b + 1), hi:far] -= plain(left(near, 0), right(near), 0, 0)

        def later(b=b, lo=lo, hi=hi, far=far, near=near, upper=upper):
            panels = [] if near is None else [(hi, near)]
            if far < n:
                rest = upper(far, n)
                panels.append((far, rest))
                s_ref[hi:far, far:] -= plain(left(near, 0), right(rest), 0, 0)
                for r in range(0, n - far, BLOCK):
                    s_ref[far + r : far + r + BLOCK, far + r :] -= plain(
                        left([p[:, r : r + BLOCK] for p in rest], 0),
                        right([p[:, r:] for p in rest]), 0, 0,
                    )
            panels.append((lo, upper(lo, hi)))
            if b == 0:
                copy.wait()
            xh, xm, _ = thirds(x_ref[:, lo:hi])
            x = jnp.concatenate([xh, xm, xh], axis=1)
            for start, (uh, um, _) in panels:
                product = plain(x, jnp.concatenate([uh, uh, um], axis=0))
                columns = slice(start, start + uh.shape[1])
                y_ref[:, columns] = product if b == 0 else y_ref[:, columns] + product

    later()


def finish_kernel(
    valid_ref, own_ref, other_ref, values_hbm, out_ref, strengths_ref, g_ref, values_ref, sem
):
    copy = pltpu.make_async_copy(values_hbm, values_ref, sem)
    copy.start()
    modes, n = strengths_ref.shape[1], values_ref.shape[1]
    nb = n // BLOCK
    packed = own_ref.shape[0] - nb * modes
    first = lax.axis_index("field") == 0

    def fill(f):

        def read(part, start, rows):
            start += part * (packed // 4)
            a = own_ref[start : start + rows, :]
            b = other_ref[start : start + rows, :]
            return jnp.where(first, a, b) if f == 0 else jnp.where(first, b, a)

        def put(i, j, v):
            g_ref[f, span(i), span(j)] = v
            if i != j:
                g_ref[f, span(j), span(i)] = v.T

        unpack(read, nb, put)

    def normal(product):
        wide = jnp.concatenate([product, jnp.zeros((modes, BLOCK - modes), F32)], axis=1)
        tiles = [wide[r : r + TILE, :] for r in range(0, modes, TILE)]
        return jnp.concatenate(inverse_factor(tiles, modes), axis=0)[:, :modes]

    y = jnp.where(first, other_ref[packed:, :], own_ref[packed:, :])
    y = jnp.concatenate([y[r : r + modes] for r in range(0, nb * modes, modes)], axis=1)
    fill(0)
    t = two_thirds(y, g_ref[0])
    product = rows_product(y, t)
    fill(1)
    inverse = normal(product)
    q0 = two_thirds(inverse, y)
    z = two_thirds(inverse, t)
    w = two_thirds(z, g_ref[1])
    inverse = normal(rows_product(z, w))
    q1 = two_thirds(inverse, z)
    row, lane = iotas((modes, modes))
    diagonal = jnp.sum(jnp.where(row == lane, inverse, 0.0), axis=0, keepdims=True)
    strengths_ref[...] = 1.0 / diagonal
    q = jnp.where(first, q0, q1)
    high = q.astype(jnp.bfloat16)
    low = (q - high.astype(F32)).astype(jnp.bfloat16)
    both = jnp.concatenate([high, low], axis=0)
    copy.wait()
    ocean = valid_ref[0, 0]
    points = values_ref.shape[0]
    step = min(points, 256)
    for r in range(0, points, step):
        product = lax.dot_general(
            both, values_ref[r : r + step, :], (((1,), (1,)), ((), ())),
            preferred_element_type=F32,
        )
        total = product[:modes] + product[modes:]
        _, place = iotas(total.shape)
        out_ref[:, r : r + step] = jnp.where(place + r < ocean, total, 0.0)


AXES = ("field", "group", "row")


def swap(value, which):
    sizes = [lax.axis_size(a) for a in AXES]
    moves = []
    for f in range(sizes[0]):
        for g in range(sizes[1]):
            for r in range(sizes[2]):
                there = dict(zip(AXES, (f, g, r)))
                for axis, b in which(f):
                    there[axis] ^= 1 << b
                here = (f * sizes[1] + g) * sizes[2] + r
                moves.append(
                    (here, (there["field"] * sizes[1] + there["group"]) * sizes[2] + there["row"])
                )
    return lax.ppermute(value, AXES, moves)


def has_bit(which):
    def of(f):
        axis, b = which(f)
        return (lax.axis_index(axis) >> b) & 1

    return jnp.where(lax.axis_index("field") == 0, of(0), of(1))


def sum_all(value):
    sizes = {axis: lax.axis_size(axis) for axis in ("row", "group")}
    if any(n & (n - 1) for n in sizes.values()) or min(sizes.values()) < 2:
        return lax.psum(value, ("group", "row"))
    bits = {axis: n.bit_length() - 1 for axis, n in sizes.items()}
    order = [("row", 0), ("group", 0)]
    order += [(axis, b) for axis in ("row", "group") for b in range(1, bits[axis])]
    steps = [lambda f, k=k: order[(k + 2 * (1 - f)) % len(order)] for k in range(len(order))]
    me = has_bit(steps[0]) + 2 * has_bit(steps[1])

    def turned(d, first=0):
        return lambda f: [step(f) for k, step in enumerate(steps[first : first + 2]) if d >> k & 1]

    others = (3, 2, 1)
    arrived = []
    for d in others:
        piece = lax.dynamic_slice_in_dim(value, me ^ d, 1, 0)
        arrived.append(swap(piece, turned(d)))
    part = lax.dynamic_slice_in_dim(value, me, 1, 0)
    for piece in arrived:
        part = part + piece
    for first in range(2, len(steps), 2):
        ways = (1, 2, 3) if first + 1 < len(steps) else (1,)
        arrived = [swap(part, turned(d, first)) for d in ways]
        for piece in arrived:
            part = part + piece
    held = {0: part}
    for d in others:
        held[d] = swap(part, turned(d))
    parts = []
    for q in range(4):
        chosen = held[q]
        for p in range(1, 4):
            chosen = jnp.where(me == p, held[q ^ p], chosen)
        parts.append(chosen)
    return jnp.concatenate(parts, axis=0)


def per_device(anomalies, valid_rows, start_basis):
    values = anomalies[0]
    rows_here, n = values.shape
    modes = start_basis.shape[1]
    nb = n // BLOCK
    extra = -(-(1 + nb // 2) // TILE) * TILE
    packed = pl.pallas_call(
        gram_kernel,
        out_shape=jax.ShapeDtypeStruct((4, nb * nb * BLOCK // 8 + extra, BLOCK), F32),
        in_specs=[SMEM, pl.BlockSpec(memory_space=pltpu.HBM)],
        out_specs=VMEM,
        scratch_shapes=[
            pltpu.VMEM((rows_here, n), jnp.bfloat16),
            pltpu.VMEM((n, n), F32),
            pltpu.SemaphoreType.DMA,
        ],
        compiler_params=pltpu.CompilerParams(vmem_limit_bytes=GRANT),
    )(valid_rows, pltpu.with_memory_space_constraint(values, pltpu.HBM))
    mine = sum_all(packed)
    own = pl.pallas_call(
        factor_kernel,
        out_shape=jax.ShapeDtypeStruct((4 * mine.shape[1] + nb * modes, BLOCK), F32),
        in_specs=[VMEM, pl.BlockSpec(memory_space=pltpu.HBM)],
        out_specs=VMEM,
        scratch_shapes=[
            pltpu.VMEM((n, n), F32),
            pltpu.VMEM((modes, n), F32),
            pltpu.VMEM((modes, n), F32),
            pltpu.SemaphoreType.DMA,
            pltpu.SemaphoreType.DMA((4,)),
        ],
        compiler_params=pltpu.CompilerParams(vmem_limit_bytes=GRANT),
    )(mine, pltpu.with_memory_space_constraint(start_basis.T, pltpu.HBM))
    other = swap(own, lambda f: [("field", 0)])
    patterns, strengths = pl.pallas_call(
        finish_kernel,
        out_shape=(
            jax.ShapeDtypeStruct((modes, rows_here), F32),
            jax.ShapeDtypeStruct((1, modes), F32),
        ),
        in_specs=[SMEM, VMEM, VMEM, pl.BlockSpec(memory_space=pl.ANY)],
        out_specs=(VMEM, VMEM),
        scratch_shapes=[
            pltpu.VMEM((2, n, n), F32),
            pltpu.VMEM((rows_here, n), jnp.bfloat16),
            pltpu.SemaphoreType.DMA,
        ],
        compiler_params=pltpu.CompilerParams(vmem_limit_bytes=GRANT),
    )(valid_rows, own, other, values)
    return patterns.T[None], strengths[0]


def solution(mesh):
    in_specs = (P("field", ("group", "row"), None), P("field", ("group", "row")), P())
    out_specs = (P("field", ("group", "row"), None), P())
    return jax.shard_map(per_device, mesh=mesh, in_specs=in_specs, out_specs=out_specs, check_vma=False)
```

```python
import jax
import jax.numpy as jnp
from jax import lax
from jax.experimental import pallas as pl
from jax.experimental.pallas import tpu as pltpu
from jax.sharding import PartitionSpec as P


F32 = jnp.float32
BLOCK = 128
TILE = 8
HALF = 64
WIDE = 256
GRANT = 16 * 2**20
VMEM = pl.BlockSpec(memory_space=pltpu.VMEM)
SMEM = pl.BlockSpec(memory_space=pltpu.SMEM)


def thirds(x):
    high = x.astype(jnp.bfloat16)
    rest = x - high.astype(F32)
    middle = rest.astype(jnp.bfloat16)
    return high, middle, (rest - middle.astype(F32)).astype(jnp.bfloat16)


def plain(a, b, ca=1, cb=0):
    return lax.dot_general(a, b, (((ca,), (cb,)), ((), ())), preferred_element_type=F32)


def left(parts, dim):
    high, middle, low = parts
    return jnp.concatenate([high, high, middle, high, low, middle], axis=dim)


def right(parts):
    high, middle, low = parts
    return jnp.concatenate([high, middle, high, low, high, middle], axis=0)


def stacked(a, b):
    return plain(left(thirds(a), 0), right(thirds(b)), 0, 0)


def two_thirds(a, b):
    ah, am, _ = thirds(a)
    bh, bm, _ = thirds(b)
    rows = a.shape[0]
    both = plain(jnp.concatenate([ah, am], axis=0), bh)
    return both[:rows] + (both[rows:] + plain(ah, bm))


def rows_product(a, b):
    ah, am, al = thirds(a)
    bh, bm, bl = thirds(b)
    m = a.shape[0]
    p = plain(jnp.concatenate([ah, am, al], axis=0), bh, 1, 1)
    q = plain(jnp.concatenate([ah, am], axis=0), bm, 1, 1)
    return p[:m] + ((p[m : 2 * m] + q[:m]) + (p[2 * m :] + q[m:] + plain(ah, bl, 1, 1)))


def lane_copy(tile, lane):
    return jnp.broadcast_to(tile[:, lane : lane + 1], tile.shape)


def row_copy(tile, row):
    return jnp.broadcast_to(tile[row : row + 1, :], tile.shape)


def iotas(shape):
    return lax.broadcasted_iota(jnp.int32, shape, 0), lax.broadcasted_iota(jnp.int32, shape, 1)


def eliminate(tiles, base):
    tiles = list(tiles)
    steps = len(tiles)
    sub, lane = iotas((TILE, BLOCK))
    cols = [lane_copy(tiles[0], base + j) for j in range(TILE)]
    out = []
    for s in range(steps):
        k = base + TILE * s
        tile = tiles[s]
        inside = (lane >= k) & (lane < k + TILE)
        scale, low = [], {}
        for j in range(TILE):
            scale.append(lax.rsqrt(row_copy(cols[j], j)))
            column = cols[j] * scale[j]
            for i in range(j + 1, TILE):
                low[i, j] = row_copy(column, i)
            for c in range(j + 1, TILE):
                cols[c] = cols[c] - column * low[c, j]
        rows = []
        for i in range(TILE):
            row = jnp.where(inside, jnp.where(lane == k + i, 1.0, 0.0), row_copy(tile, i))
            for m in range(i):
                row = row - low[i, m] * rows[m]
            rows.append(row * scale[i])
        new = rows[0]
        for i in range(1, TILE):
            new = jnp.where(sub == i, rows[i], new)
        out.append(new)
        for g in range(s + 1, steps):
            t = tiles[g]
            w = []
            for j in range(TILE):
                acc = lane_copy(t, k + j)
                for m in range(j):
                    acc = acc - low[j, m] * w[m]
                w.append(acc * scale[j])
            if g == s + 1:
                cols = [lane_copy(t, k + TILE + c) for c in range(TILE)]
                for c in range(TILE):
                    for i in range(TILE):
                        cols[c] = cols[c] - w[i] * row_copy(w[i], c)
            t = jnp.where(inside, 0.0, t)
            for i in range(TILE):
                t = t - w[i] * rows[i]
            tiles[g] = t
    return out


def inverse_factor(tiles, size, between=lambda: None):
    tiles = list(tiles)
    out = []
    count = size // TILE
    _, lane = iotas((TILE, BLOCK))
    for base in range(0, len(tiles) * TILE, size):
        done = eliminate(tiles[:count], base)
        out += done
        if base == 0:
            between()
        tiles = tiles[count:]
        if tiles:
            rows = jnp.concatenate(done, axis=0)
            place, at = iotas(rows.shape)
            keep = (at <= place + base) | (at >= base + size)
            update = stacked(rows, jnp.where(keep, rows, 0.0))
            for g in range(len(tiles)):
                start = base + size + TILE * g
                kept = jnp.where(lane < base + size, jnp.where(lane < base, tiles[g], 0.0), tiles[g])
                tiles[g] = kept - update[start : start + TILE, :]
    sub, _ = iotas((TILE, BLOCK))
    return [jnp.where(lane <= TILE * s + sub, t, 0.0) for s, t in enumerate(out)]


def layout(nb):
    shared = [(i, i) for i in range(0, nb, 2)]
    return shared + [(i, j) for i in range(nb) for j in range(i + 1, nb)]


def gram_kernel(valid_ref, values_hbm, out_ref, values_ref, gram_ref, sem):
    copy = pltpu.make_async_copy(values_hbm, values_ref, sem)
    copy.start()
    points, n = values_ref.shape
    nb = n // BLOCK
    ocean = valid_ref[0, 0]
    place, _ = iotas((points, n))
    copy.wait()
    masked = jnp.where(place < ocean, values_ref[...].astype(F32), 0.0).astype(jnp.bfloat16)
    for start in range(0, n, WIDE):
        stop = min(start + WIDE, n)
        gram_ref[start:stop, start:] = plain(masked[:, start:stop], masked[:, start:], 0, 0)
    row, lane = iotas((BLOCK, BLOCK))
    quarter = nb * nb * BLOCK // 8
    extra = [jnp.full((1, BLOCK), ocean.astype(F32))]
    for t, (i, j) in enumerate(layout(nb)):
        block = gram_ref[span(i), span(j)]
        if i == j:
            second = gram_ref[span(i + 1), span(i + 1)]
            block = jnp.where(row <= lane, block, second)
            extra.append(jnp.sum(jnp.where(row == lane, second, 0.0), axis=0, keepdims=True))
        half = BLOCK // 2
        for h in range(2):
            part, offset = divmod(t * BLOCK + half * h, quarter)
            out_ref[part, offset : offset + half, :] = block[half * h : half * (h + 1)]
    fill = jnp.zeros((-len(extra) % TILE, BLOCK), F32)
    extra = jnp.concatenate(extra + [fill], axis=0)
    for part in range(4):
        out_ref[part, quarter:, :] = extra


def unpack(read, nb, put):
    quarter = nb * nb * BLOCK // 8
    row, lane = iotas((BLOCK, BLOCK))
    inverse = 1.0 / read(0, quarter, 1)

    def block(t):
        halves = []
        for start in (t * BLOCK, t * BLOCK + BLOCK // 2):
            part, offset = divmod(start, quarter)
            halves.append(read(part, offset, BLOCK // 2) * inverse)
        return jnp.concatenate(halves, axis=0)

    for t, (i, j) in enumerate(layout(nb)):
        if i == j:
            both = block(t)
            turned = both.T
            ends = read(0, quarter + 1 + i // 2, 1) * inverse
            put(i, i, jnp.where(row <= lane, both, turned))
            second = jnp.where(row > lane, both, turned)
            put(i + 1, i + 1, jnp.where(row == lane, ends, second))
        else:
            put(i, j, block(t))


def span(i):
    return slice(i * BLOCK, (i + 1) * BLOCK)


def factor_kernel(mine_ref, x_hbm, y_ref, s_ref, x_ref, sem):
    @pl.when(lax.axis_index("field") == 0)
    def _():
        y_ref[...] = jnp.zeros_like(y_ref)

    @pl.when(lax.axis_index("field") == 1)
    def _():
        apply_factor(mine_ref, x_hbm, y_ref, s_ref, x_ref, sem)


def apply_factor(mine_ref, x_hbm, y_ref, s_ref, x_ref, sem):
    copy = pltpu.make_async_copy(x_hbm, x_ref, sem)
    copy.start()
    n = x_ref.shape[1]
    nb = n // BLOCK

    def read(part, start, rows):
        return mine_ref[part, start : start + rows, :]

    def put(i, j, v):
        s_ref[span(i), span(j)] = v

    unpack(read, nb, put)
    later = lambda: None
    for b in range(nb):
        lo, hi = b * BLOCK, (b + 1) * BLOCK
        far = hi + BLOCK
        tiles = [s_ref[lo + r : lo + r + TILE, lo:hi] for r in range(0, BLOCK, TILE)]
        inverse = jnp.concatenate(inverse_factor(tiles, HALF, later), axis=0)
        inverse = left(thirds(inverse), 1)

        def upper(start, stop, inverse=inverse, lo=lo, hi=hi):
            return thirds(plain(inverse, right(thirds(s_ref[lo:hi, start:stop]))))

        near = None
        if hi < n:
            near = upper(hi, far)
            s_ref[span(b + 1), hi:far] -= plain(left(near, 0), right(near), 0, 0)

        def later(b=b, lo=lo, hi=hi, far=far, near=near, upper=upper):
            panels = [] if near is None else [(hi, near)]
            if far < n:
                rest = upper(far, n)
                panels.append((far, rest))
                s_ref[hi:far, far:] -= plain(left(near, 0), right(rest), 0, 0)
                for r in range(0, n - far, BLOCK):
                    s_ref[far + r : far + r + BLOCK, far + r :] -= plain(
                        left([p[:, r : r + BLOCK] for p in rest], 0),
                        right([p[:, r:] for p in rest]), 0, 0,
                    )
            panels.append((lo, upper(lo, hi)))
            if b == 0:
                copy.wait()
            xh, xm, _ = thirds(x_ref[:, lo:hi])
            x = jnp.concatenate([xh, xm, xh], axis=1)
            for start, (uh, um, _) in panels:
                product = plain(x, jnp.concatenate([uh, uh, um], axis=0))
                columns = slice(start, start + uh.shape[1])
                y_ref[:, columns] = product if b == 0 else y_ref[:, columns] + product

    later()


def finish_kernel(
    valid_ref, mine_ref, other_ref, y_ref, y_other_ref, values_hbm, out_ref, strengths_ref,
    g_ref, values_ref, sem,
):
    copy = pltpu.make_async_copy(values_hbm, values_ref, sem)
    copy.start()
    modes, n = y_ref.shape
    nb = n // BLOCK
    first = lax.axis_index("field") == 0

    def fill(f):

        def read(part, start, rows):
            a = mine_ref[part, start : start + rows, :]
            b = other_ref[part, start : start + rows, :]
            return jnp.where(first, a, b) if f == 0 else jnp.where(first, b, a)

        def put(i, j, v):
            g_ref[f, span(i), span(j)] = v
            if i != j:
                g_ref[f, span(j), span(i)] = v.T

        unpack(read, nb, put)

    def normal(product):
        wide = jnp.concatenate([product, jnp.zeros((modes, BLOCK - modes), F32)], axis=1)
        tiles = [wide[r : r + TILE, :] for r in range(0, modes, TILE)]
        return jnp.concatenate(inverse_factor(tiles, modes), axis=0)[:, :modes]

    y = jnp.where(first, y_other_ref[...], y_ref[...])
    fill(0)
    t = two_thirds(y, g_ref[0])
    product = rows_product(y, t)
    fill(1)
    inverse = normal(product)
    q0 = two_thirds(inverse, y)
    z = two_thirds(inverse, t)
    w = two_thirds(z, g_ref[1])
    inverse = normal(rows_product(z, w))
    q1 = two_thirds(inverse, z)
    row, lane = iotas((modes, modes))
    diagonal = jnp.sum(jnp.where(row == lane, inverse, 0.0), axis=0, keepdims=True)
    strengths_ref[...] = 1.0 / diagonal
    q = jnp.where(first, q0, q1)
    high = q.astype(jnp.bfloat16)
    low = (q - high.astype(F32)).astype(jnp.bfloat16)
    both = jnp.concatenate([high, low], axis=0)
    copy.wait()
    ocean = valid_ref[0, 0]
    points = values_ref.shape[0]
    step = min(points, 256)
    for r in range(0, points, step):
        product = lax.dot_general(
            both, values_ref[r : r + step, :], (((1,), (1,)), ((), ())),
            preferred_element_type=F32,
        )
        total = product[:modes] + product[modes:]
        _, place = iotas(total.shape)
        out_ref[:, r : r + step] = jnp.where(place + r < ocean, total, 0.0)


AXES = ("field", "group", "row")


def swap(value, which):
    sizes = [lax.axis_size(a) for a in AXES]
    moves = []
    for f in range(sizes[0]):
        for g in range(sizes[1]):
            for r in range(sizes[2]):
                there = dict(zip(AXES, (f, g, r)))
                for axis, b in which(f):
                    there[axis] ^= 1 << b
                here = (f * sizes[1] + g) * sizes[2] + r
                moves.append(
                    (here, (there["field"] * sizes[1] + there["group"]) * sizes[2] + there["row"])
                )
    return lax.ppermute(value, AXES, moves)


def has_bit(which):
    def of(f):
        axis, b = which(f)
        return (lax.axis_index(axis) >> b) & 1

    return jnp.where(lax.axis_index("field") == 0, of(0), of(1))


def sum_all(value):
    sizes = {axis: lax.axis_size(axis) for axis in ("row", "group")}
    if any(n & (n - 1) for n in sizes.values()) or min(sizes.values()) < 2:
        return lax.psum(value, ("group", "row"))
    bits = {axis: n.bit_length() - 1 for axis, n in sizes.items()}
    order = [("row", 0), ("group", 0)]
    order += [(axis, b) for axis in ("row", "group") for b in range(1, bits[axis])]
    steps = [lambda f, k=k: order[(k + 2 * (1 - f)) % len(order)] for k in range(len(order))]
    me = has_bit(steps[0]) + 2 * has_bit(steps[1])

    def turned(d, first=0):
        return lambda f: [step(f) for k, step in enumerate(steps[first : first + 2]) if d >> k & 1]

    others = (3, 2, 1)
    arrived = []
    for d in others:
        piece = lax.dynamic_slice_in_dim(value, me ^ d, 1, 0)
        arrived.append(swap(piece, turned(d)))
    part = lax.dynamic_slice_in_dim(value, me, 1, 0)
    for piece in arrived:
        part = part + piece
    for first in range(2, len(steps), 2):
        ways = (1, 2, 3) if first + 1 < len(steps) else (1,)
        arrived = []
        for d in ways:
            arrived.append(swap(part, turned(d, first)))
        for piece in arrived:
            part = part + piece
    held = {0: part}
    for d in others:
        held[d] = swap(part, turned(d))
    parts = []
    for q in range(4):
        chosen = held[q]
        for p in range(1, 4):
            chosen = jnp.where(me == p, held[q ^ p], chosen)
        parts.append(chosen)
    return jnp.concatenate(parts, axis=0)


def per_device(anomalies, valid_rows, start_basis):
    values = anomalies[0]
    rows_here, n = values.shape
    modes = start_basis.shape[1]
    nb = n // BLOCK
    extra = -(-(1 + nb // 2) // TILE) * TILE
    packed = pl.pallas_call(
        gram_kernel,
        out_shape=jax.ShapeDtypeStruct((4, nb * nb * BLOCK // 8 + extra, BLOCK), F32),
        in_specs=[SMEM, pl.BlockSpec(memory_space=pltpu.HBM)],
        out_specs=VMEM,
        scratch_shapes=[
            pltpu.VMEM((rows_here, n), jnp.bfloat16),
            pltpu.VMEM((n, n), F32),
            pltpu.SemaphoreType.DMA,
        ],
        compiler_params=pltpu.CompilerParams(vmem_limit_bytes=GRANT),
    )(valid_rows, pltpu.with_memory_space_constraint(values, pltpu.HBM))
    mine = sum_all(packed)
    y = pl.pallas_call(
        factor_kernel,
        out_shape=jax.ShapeDtypeStruct((modes, n), F32),
        in_specs=[VMEM, pl.BlockSpec(memory_space=pltpu.HBM)],
        out_specs=VMEM,
        scratch_shapes=[
            pltpu.VMEM((n, n), F32),
            pltpu.VMEM((modes, n), F32),
            pltpu.SemaphoreType.DMA,
        ],
        compiler_params=pltpu.CompilerParams(vmem_limit_bytes=GRANT),
    )(mine, pltpu.with_memory_space_constraint(start_basis.T, pltpu.HBM))
    y, mine = lax.optimization_barrier((y, mine))
    partner = lambda f: [("field", 0)]
    y_other = swap(y, partner)
    other = swap(mine, partner)
    patterns, strengths = pl.pallas_call(
        finish_kernel,
        out_shape=(
            jax.ShapeDtypeStruct((modes, rows_here), F32),
            jax.ShapeDtypeStruct((1, modes), F32),
        ),
        in_specs=[SMEM, VMEM, VMEM, VMEM, VMEM, pl.BlockSpec(memory_space=pl.ANY)],
        out_specs=(VMEM, VMEM),
        scratch_shapes=[
            pltpu.VMEM((2, n, n), F32),
            pltpu.VMEM((rows_here, n), jnp.bfloat16),
            pltpu.SemaphoreType.DMA,
        ],
        compiler_params=pltpu.CompilerParams(vmem_limit_bytes=GRANT),
    )(valid_rows, mine, other, y, y_other, values)
    return patterns.T[None], strengths[0]


def solution(mesh):
    in_specs = (P("field", ("group", "row"), None), P("field", ("group", "row")), P())
    out_specs = (P("field", ("group", "row"), None), P())
    return jax.shard_map(per_device, mesh=mesh, in_specs=in_specs, out_specs=out_specs, check_vma=False)
```
